32 devices in a mesh: row: 8 (over y, x, core), col: 4 (over z).
Axes of the slice: x: 2, y: 2, z: 4, core: 2. Of those that a mesh axis runs over, the one named last changes fastest.
Arguments:
- pooled: bfloat16 [4096, 1152], P(('row', 'col')), may hold values from -6 to 6
- text_embed: bfloat16 [4096, 1152], P(('row', 'col')), may hold values from -0.29882812 to 0.29882812
- head_weight: bfloat16 [1152, 1152], replicated, may hold values from -0.1875 to 0.1875
- logit_scale: float32 [4], replicated, may hold values from 1 to 4
- logit_bias: float32 [4], replicated, may hold values from -2 to 0
- partner: int32 [32, 128], P(('row', 'col')), may hold values from 0 to 127, each once within a row
Outputs:
- text_grad: float32 [4096, 1152], P(('row', 'col'))
- head_grad: float32 [1152, 1152], P('row', 'col')
The draws below stay inside these ranges and needn't reach their ends.
Inputs may be any that keep to these rules, and one draw needn't show every extreme that they name: Each row of partner is a permutation of the indices within a block.
All inputs are finite; a program needn't handle non-finite values.
Results may differ from the reference program's by a relative error of at most 0.004.
Values may be sent and summed in bfloat16 or wider, within the bound.
A program may use at most 64 MiB of HBM per device.

```python
import math
import jax
import jax.numpy as jnp
from jax import lax

D = 1152
PAIRS_DEV = 128
BLOCKS = 32
PAIRS = 4096
N_ROW = 8
N_COL = 4


def level_of(key, shape, cuts, least, top_value):
    level, own = 1.0, jax.random.fold_in(key, 6)
    for position, shards_of in cuts:
        heights = jnp.exp(jax.random.uniform(jax.random.fold_in(own, position), (shards_of,), jnp.float32, least / len(cuts), top_value / len(cuts)))
        level = level * jnp.repeat(heights, shape[position] // shards_of).reshape([-1 if axis == position else 1 for axis in range(len(shape))])
    return level


def noise(stream_key, shape, spread, bound, pieces=(), kind=jnp.bfloat16):
    array = jax.random.normal(stream_key, shape, jnp.float32) * spread
    if len(pieces) > 0:
        array = level_of(stream_key, shape, pieces, -0.22, 0.18) * array
    return jnp.clip(array, min=-bound, max=bound).astype(kind)


def setup_inputs(seed: int = 0) -> dict:
    arg_keys = jax.random.split(jax.random.key(seed), 7)
    return {
        "pooled": noise(arg_keys[0], (PAIRS, D), 1.0, 6.0, ((0, 32),)),
        "text_embed": noise(arg_keys[1], (PAIRS, D), 0.05, 0.29882812, ((0, 32),)),
        "head_weight": noise(arg_keys[2], (D, D), D ** -0.5, 0.1875),
        "logit_scale": jnp.clip(jnp.exp(jax.random.uniform(arg_keys[3], (4,), jnp.float32, math.log(1.0), math.log(4.0))), 1.0, 4.0),
        "logit_bias": jnp.clip(jax.random.uniform(arg_keys[4], (4,), jnp.float32, -2.0, 0.0), -2.0, 0.0),
        "partner": jax.vmap(lambda own: jax.random.permutation(own, PAIRS_DEV))(jax.random.split(arg_keys[5], BLOCKS)).reshape((BLOCKS, PAIRS_DEV)).astype(jnp.int32),
    }


def segment_weights(image_part, text_part, positive, logit_scale, logit_bias, factor):
    model_width = image_part.shape[1]
    bounds = [0, model_width // 8, model_width // 4, model_width // 2, model_width]
    running = jnp.zeros((image_part.shape[0], text_part.shape[0]), jnp.float32)
    level_grads = []
    for prefix in range(4):
        low_end = bounds[prefix]
        high_end = bounds[prefix + 1]
        running = running + jnp.dot(image_part[:, low_end:high_end], text_part[:, low_end:high_end].T, preferred_element_type=jnp.float32)
        logits = logit_scale[prefix] * running + logit_bias[prefix]
        level_grads.append((jax.nn.sigmoid(logits) - positive) * factor)
    weights = []
    carried = jnp.zeros_like(running)
    for prefix in range(3, -1, -1):
        carried = carried + logit_scale[prefix] * level_grads[prefix]
        weights.insert(0, carried.astype(jnp.bfloat16))
    return (weights, bounds)

def apply_weights(weights, bounds, image_part, text_part):
    image_pieces = []
    text_pieces = []
    for prefix in range(4):
        low_end = bounds[prefix]
        high_end = bounds[prefix + 1]
        image_pieces.append(jnp.dot(weights[prefix], text_part[:, low_end:high_end], preferred_element_type=jnp.float32))
        text_pieces.append(jnp.dot(weights[prefix].T, image_part[:, low_end:high_end], preferred_element_type=jnp.float32))
    return (jnp.concatenate(image_pieces, 1), jnp.concatenate(text_pieces, 1))

def reference(pooled, text_embed, head_weight, logit_scale, logit_bias, partner):
    pair_count = pooled.shape[0]
    model_width = pooled.shape[1]
    block_rows = partner.shape[1]
    factor = 1.0 / math.sqrt(pair_count)
    embedding = jnp.dot(pooled, head_weight, preferred_element_type=jnp.float32).astype(jnp.bfloat16)
    shape_four = (N_ROW, N_COL, block_rows, model_width)
    emb_blocks = embedding.reshape(shape_four)
    emb_ahead = jnp.roll(emb_blocks, -1, axis=0)
    pooled_blocks = pooled.reshape(shape_four)
    pooled_ahead = jnp.roll(pooled_blocks, -1, axis=0)
    text_blocks = text_embed.reshape(shape_four)
    partner_blocks = partner.reshape(N_ROW, N_COL, block_rows)
    local_ids = jnp.arange(block_rows, dtype=jnp.int32)

    def one_block(emb_own, emb_next, text_own, partner_own):
        positive = (partner_own[:, None] == local_ids[None, :]).astype(jnp.float32)
        weights, bounds = segment_weights(emb_own, text_own, positive, logit_scale, logit_bias, factor)
        own_image, own_text = apply_weights(weights, bounds, emb_own, text_own)
        empty = jnp.zeros((block_rows, block_rows), jnp.float32)
        weights, bounds = segment_weights(emb_next, text_own, empty, logit_scale, logit_bias, factor)
        next_image, next_text = apply_weights(weights, bounds, emb_next, text_own)
        return (own_image, next_image, own_text + next_text)

    def advance(carry, inputs):
        emb_own, emb_next, text_own, partner_own, pool_own, pool_next = inputs
        own_image, next_image, text_terms = jax.vmap(one_block)(emb_own, emb_next, text_own, partner_own)
        flat_own = pool_own.reshape(-1, model_width).astype(jnp.float32)
        flat_next = pool_next.reshape(-1, model_width).astype(jnp.float32)
        carry = carry + jnp.dot(flat_own.T, own_image.reshape(-1, model_width), precision=lax.Precision.HIGHEST)
        carry = carry + jnp.dot(flat_next.T, next_image.reshape(-1, model_width), precision=lax.Precision.HIGHEST)
        return (carry, text_terms)
    start_grad = jnp.zeros((model_width, model_width), jnp.float32)
    head_grad, text_terms = lax.scan(advance, start_grad, (emb_blocks, emb_ahead, text_blocks, partner_blocks, pooled_blocks, pooled_ahead))
    text_grad = text_terms.reshape(pair_count, model_width)
    return (text_grad, head_grad)
```

```python
import functools
import math

import jax
import jax.numpy as jnp
from jax import lax
from jax.experimental import pallas as pl
from jax.experimental.pallas import tpu as pltpu
from jax.sharding import PartitionSpec as P

LANES = 128
MESH = pl.DeviceIdType.MESH


def shifted(value, axis, by):
    count = lax.axis_size(axis)
    return lax.ppermute(value, axis, [(i, (i + by) % count) for i in range(count)])


def segment_weights(image_part, text_part, positive, logit_scale, logit_bias, factor):
    model_width = image_part.shape[1]
    bounds = [0, model_width // 8, model_width // 4, model_width // 2, model_width]
    running = jnp.zeros((image_part.shape[0], text_part.shape[0]), jnp.float32)
    level_grads = []
    for prefix in range(4):
        low_end = bounds[prefix]
        high_end = bounds[prefix + 1]
        running = running + jnp.dot(
            image_part[:, low_end:high_end],
            text_part[:, low_end:high_end].T,
            preferred_element_type=jnp.float32,
        )
        logits = logit_scale[prefix] * running + logit_bias[prefix]
        level_grads.append((jax.nn.sigmoid(logits) - positive) * factor)
    weights = []
    carried = jnp.zeros_like(running)
    for prefix in range(3, -1, -1):
        carried = carried + logit_scale[prefix] * level_grads[prefix]
        weights.insert(0, carried.astype(jnp.bfloat16))
    return (weights, bounds)


def image_side(weights, bounds, text_part):
    pieces = []
    for prefix in range(4):
        pieces.append(
            jnp.dot(
                weights[prefix],
                text_part[:, bounds[prefix] : bounds[prefix + 1]],
                preferred_element_type=jnp.float32,
            )
        )
    return jnp.concatenate(pieces, 1)


def text_side(weights, bounds, image_part):
    pieces = []
    for prefix in range(4):
        pieces.append(
            jnp.dot(
                weights[prefix].T,
                image_part[:, bounds[prefix] : bounds[prefix + 1]],
                preferred_element_type=jnp.float32,
            )
        )
    return jnp.concatenate(pieces, 1)


def body(pooled, text_embed, head_weight, logit_scale, logit_bias, partner):
    block_rows = pooled.shape[0]
    factor = 1.0 / math.sqrt(block_rows * lax.axis_size("row") * lax.axis_size("col"))
    embedding = jnp.dot(pooled, head_weight, preferred_element_type=jnp.float32).astype(
        jnp.bfloat16
    )
    local_ids = jnp.arange(block_rows, dtype=jnp.int32)
    positive = (partner[0][:, None] == local_ids[None, :]).astype(jnp.float32)
    empty = jnp.zeros((block_rows, block_rows), jnp.float32)
    weights, bounds = segment_weights(
        embedding, text_embed, positive, logit_scale, logit_bias, factor
    )
    own_image = image_side(weights, bounds, text_embed)
    own_text = text_side(weights, bounds, embedding)
    behind = shifted(text_embed, "row", 1)
    weights, bounds = segment_weights(embedding, behind, empty, logit_scale, logit_bias, factor)
    cross_image = image_side(weights, bounds, behind)
    cross_text = text_side(weights, bounds, embedding)
    returned = shifted(cross_text.astype(jnp.bfloat16), "row", -1).astype(cross_text.dtype)
    text_grad = own_text + returned
    image_grad = own_image + cross_image
    column_block = lax.all_to_all(
        image_grad.astype(jnp.bfloat16), "col", split_axis=1, concat_axis=0, tiled=True
    ).astype(image_grad.dtype)
    group_rows = lax.all_gather(pooled, "col", axis=0, tiled=True)
    block_term = jnp.dot(
        group_rows.astype(jnp.float32).T, column_block, precision=lax.Precision.HIGHEST
    )
    head_grad = lax.psum_scatter(block_term, "row", scatter_dimension=0, tiled=True)
    return (text_grad, head_grad)


def dot_nt(left, right):
    return lax.dot_general(
        left, right, (((1,), (1,)), ((), ())), preferred_element_type=jnp.float32
    )


def dot_nn(left, right):
    return jnp.dot(left, right, preferred_element_type=jnp.float32)


def aligned(low_end, high_end):
    return low_end // LANES * LANES, -(-high_end // LANES) * LANES


def weights_of(score_of, positive, scale_ref, bias_ref, factor):
    running = None
    level_grads = []
    for prefix in range(4):
        part = score_of(prefix)
        running = part if running is None else running + part
        gate = jax.nn.sigmoid(scale_ref[prefix] * running + bias_ref[prefix])
        if positive is not None:
            gate = gate - positive
        level_grads.append(gate * factor)
    weights = [None] * 4
    carried = None
    for prefix in range(3, -1, -1):
        term = scale_ref[prefix] * level_grads[prefix]
        carried = term if carried is None else carried + term
        weights[prefix] = carried.astype(jnp.bfloat16)
    return weights


def by_tile(piece_of, bounds, store):
    pieces = []
    for q in range(4):
        start, stop = aligned(bounds[q], bounds[q + 1])
        pieces.append((start, stop, piece_of(q, start, stop)))
    for tile in range(bounds[4] // LANES):
        base = tile * LANES
        value = None
        for q in range(4):
            start, stop, piece = pieces[q]
            if start <= base < stop:
                here = piece[:, base - start : base - start + LANES]
                if value is None:
                    value = here
                else:
                    lane = lax.broadcasted_iota(jnp.int32, here.shape, 1)
                    value = jnp.where(lane < bounds[q] - base, value, here)
        store(base, value)


def kernel(
    n_row,
    n_col,
    factor,
    chunks,
    ready,
    window,
    tail_rows,
    pooled_hbm,
    text_hbm,
    weight_hbm,
    scale_hbm,
    bias_hbm,
    partner_hbm,
    text_grad_ref,
    head_grad_ref,
    pooled_ref,
    text_ref,
    weight_ref,
    scale_ref,
    bias_ref,
    partner_ref,
    load_sem,
    image_own,
    cross_text,
    text_back,
    text_behind,
    pooled_t,
    pooled_cols,
    embed,
    masked,
    image,
    total,
    sent,
    landed,
    near_send,
    near_recv,
    pool_send,
    pool_recv,
    image_send,
    image_recv,
    out_send,
    out_recv,
):
    rows, width = pooled_hbm.shape
    chips = n_row // 2
    head_rows = width // n_row
    head_cols = width // n_col
    bounds = [0, width // 8, width // 4, width // 2, width]
    row = lax.axis_index("row")
    col = lax.axis_index("col")
    chip = row // 2
    core = row % 2

    side = chip % 2
    level = chip // 2

    def peer(k, e):
        there = chip + (k % 2) * (1 - 2 * side) + (k // 2) * (2 - 4 * level)
        return there * 2 + (core if e == 0 else 1 - core)

    barrier = pltpu.get_barrier_semaphore()
    for d in range(1, n_row):
        pl.semaphore_signal(
            barrier, inc=1, device_id=((row + d) % n_row, col), device_id_type=MESH
        )
    for d in range(1, n_col):
        pl.semaphore_signal(
            barrier, inc=1, device_id=(row, (col + d) % n_col), device_id_type=MESH
        )

    loads = [
        pltpu.make_async_copy(src, dst, load_sem.at[n])
        for n, (src, dst) in enumerate(
            (
                (pooled_hbm, pooled_ref),
                (weight_hbm, weight_ref),
                (text_hbm, text_ref),
                (scale_hbm, scale_ref),
                (bias_hbm, bias_ref),
                (partner_hbm, partner_ref),
            )
        )
    ]
    for load in loads:
        load.start()

    def remote(src, dst, send, recv, device):
        return pltpu.make_async_remote_copy(
            src_ref=src,
            dst_ref=dst,
            send_sem=send,
            recv_sem=recv,
            device_id=device,
            device_id_type=MESH,
        )

    behind_copy = remote(
        text_hbm, text_behind, near_send.at[0], near_recv.at[0], ((row + 1) % n_row, col)
    )
    back_copy = remote(
        cross_text,
        text_back,
        near_send.at[1],
        near_recv.at[1],
        ((row + n_row - 1) % n_row, col),
    )
    pl.semaphore_wait(barrier, n_row + n_col - 2)
    behind_copy.start()
    loads[0].wait()

    for tile in range(width // LANES):
        lanes = pl.ds(tile * LANES, LANES)
        pooled_t[lanes, :] = pooled_ref[:, lanes].T
    pool_copies = []
    for k in range(chips):
        for e in range(2):
            slot = 2 * k + e
            if slot == 0:
                continue
            target = peer(k, e)
            copy = remote(
                pooled_t.at[pl.ds(pl.multiple_of(target * head_rows, 16), head_rows), :],
                pooled_cols.at[:, pl.ds(slot * rows, rows)],
                pool_send.at[slot],
                pool_recv.at[slot],
                (target, col),
            )
            pool_copies.append(copy)
    pooled_cols[:, pl.ds(0, rows)] = pooled_t[
        pl.ds(pl.multiple_of(row * head_rows, 16), head_rows), :
    ]

    def fill_embed(source):
        at = 0
        for q in range(4):
            start, stop = aligned(bounds[q], bounds[q + 1])
            at += stop - start
        step = 3 * LANES if width % (3 * LANES) == 0 else LANES
        for base in range(0, width, step):
            part = dot_nn(source[...], weight_ref[:, pl.ds(base, step)])
            embed[:, pl.ds(base, step)] = part.astype(jnp.bfloat16)
        at = 0
        for q in range(4):
            start, stop = aligned(bounds[q], bounds[q + 1])
            part = embed[:, pl.ds(start, stop - start)].astype(jnp.float32)
            lane = lax.broadcasted_iota(jnp.int32, part.shape, 1) + start
            keep = (lane >= bounds[q]) & (lane < bounds[q + 1])
            masked[:, pl.ds(at, stop - start)] = jnp.where(keep, part, 0.0).astype(
                jnp.bfloat16
            )
            at += stop - start

    def masked_part(q):
        at = 0
        for before in range(q):
            start, stop = aligned(bounds[before], bounds[before + 1])
            at += stop - start
        start, stop = aligned(bounds[q], bounds[q + 1])
        return masked[:, pl.ds(at, stop - start)]

    def text_part(ref, q):
        start, stop = aligned(bounds[q], bounds[q + 1])
        return ref[:, pl.ds(start, stop - start)]

    for copy in pool_copies:
        copy.start()
    loads[1].wait()
    fill_embed(pooled_ref)
    for load in loads[2:]:
        load.wait()
    text_id = lax.broadcasted_iota(jnp.int32, (rows, rows), 0)
    positive = (text_id == partner_ref[...]).astype(jnp.float32).T
    own = weights_of(
        lambda q: dot_nt(masked_part(q), text_part(text_ref, q)),
        positive,
        scale_ref,
        bias_ref,
        factor,
    )

    def own_image_piece(q, start, stop):
        return dot_nn(own[q], text_ref[:, pl.ds(start, stop - start)])

    def keep_image(base, value):
        image_own[:, pl.ds(base, LANES)] = value

    by_tile(own_image_piece, bounds, keep_image)

    def own_text_piece(q, start, stop):
        return dot_nn(own[q].T, embed[:, pl.ds(start, stop - start)])

    def store_text(base, value):
        text_grad_ref[:, pl.ds(base, LANES)] = value

    by_tile(own_text_piece, bounds, store_text)

    behind_copy.wait_recv()
    cross = weights_of(
        lambda q: dot_nt(masked_part(q), text_part(text_behind, q)),
        None,
        scale_ref,
        bias_ref,
        factor,
    )

    def image_piece(q, start, stop):
        lanes = pl.ds(start, stop - start)
        return dot_nn(cross[q], text_behind[:, lanes])

    def store_image(base, value):
        lanes = pl.ds(base, LANES)
        image[pl.ds(0, rows), lanes] = (image_own[:, lanes] + value).astype(jnp.bfloat16)

    by_tile(image_piece, bounds, store_image)

    chunk = width // chunks
    half = rows // 2
    flip = (2 * col >= n_col).astype(jnp.int32)

    def mirrored(index, count):
        return flip * index + (1 - flip) * (count - 1 - index)

    def piece_of(slot, i, first=0, count=rows):
        lanes = pl.ds(pl.multiple_of(mirrored(i, chunks) * chunk, LANES), chunk)
        return image.at[pl.ds(slot * rows + first, count), lanes]

    image_copies = {}

    def send_image(name, src_slot, dst_slot, i, target, first=0, count=rows):
        image_copies[name, i] = remote(
            piece_of(src_slot, i, first, count),
            piece_of(dst_slot, i, first, count),
            image_send.at[name, i],
            image_recv.at[name, i],
            (target, col),
        )
        image_copies[name, i].start()

    def send_own(i):
        send_image(2, 0, 2, i, peer(1, 0))
        send_image(4, 0, 4, i, peer(2, 0))
        send_image(1, 0, 1, i, peer(0, 1))

    def pass_direct(i):
        image_copies[2, i].wait_recv()
        send_image(6, 2, 6, i, peer(2, 0), 0, half)
        send_image(3, 2, 3, i, peer(0, 1))
        image_copies[4, i].wait_recv()
        send_image(8, 4, 6, i, peer(1, 0), half, half)
        send_image(5, 4, 5, i, peer(0, 1))

    def pass_corner(i):
        image_copies[6, i].wait_recv()
        image_copies[8, i].wait_recv()
        send_image(7, 6, 7, i, peer(0, 1))

    for i in range(chunks - 1):
        send_own(i)

    def cross_text_piece(q, start, stop):
        return dot_nn(cross[q].T, embed[:, pl.ds(start, stop - start)])

    def store_cross(base, value):
        cross_text[:, pl.ds(base, LANES)] = value.astype(jnp.bfloat16)

    by_tile(cross_text_piece, bounds, store_cross)

    pass_direct(0)
    send_own(chunks - 1)
    pass_corner(0)
    for i in range(1, chunks):
        pass_direct(i)
    for i in range(1, chunks - 1):
        pass_corner(i)
    back_copy.start()

    main = head_cols // LANES * LANES
    tail = head_cols - main
    groups = head_rows // tail_rows

    def lanes_of(block):
        first = block * head_cols // LANES * LANES
        offset = block * head_cols - first
        part = total[:, pl.ds(pl.multiple_of(first, LANES), window)]
        return pltpu.roll(part, (window - offset) % window, 1)

    def packed(block):
        part = lanes_of(block)
        parts = [part[:, base : base + LANES] for base in range(0, main, LANES)]
        if tail:
            last = part[:, main : main + LANES]
            lane = lax.broadcasted_iota(jnp.int32, last.shape, 1)
            last = jnp.where(lane < tail, last, 0.0)
            joined = last[:tail_rows]
            for j in range(1, groups):
                here = last[j * tail_rows : (j + 1) * tail_rows]
                joined = joined + pltpu.roll(here, j * tail, 1)
            parts.append(joined)
        return parts

    def out_copy(block):
        return remote(
            sent.at[block],
            landed.at[col],
            out_send.at[block],
            out_recv.at[col],
            (row, block),
        )

    def in_copy(block):
        return remote(
            sent.at[block],
            landed.at[block],
            out_send.at[block],
            out_recv.at[block],
            (row, block),
        )

    for copy in pool_copies:
        copy.wait_recv()
    done = 0
    for i in range(chunks):
        if i == chunks - 1:
            pass_corner(i)
        image_copies[1, i].wait_recv()
        for slot in (3, 5, 7):
            image_copies[slot, i].wait_recv()
        lanes = pl.ds(pl.multiple_of(mirrored(i, chunks) * chunk, LANES), chunk)
        total[:, lanes] = dot_nn(pooled_cols[...], image[:, lanes])
        while done < n_col and ready[done] <= (i + 1) * chunk:
            block = mirrored(done, n_col)

            @pl.when(block != col)
            def _():
                at = 0
                for part in packed(block):
                    count = part.shape[0]
                    sent[block, pl.ds(at, count), :] = part.astype(jnp.bfloat16)
                    at += count
                out_copy(block).start()

            done += 1

    back_copy.wait_recv()
    text_grad_ref[...] = text_grad_ref[...] + text_back[...].astype(jnp.float32)

    results = packed(col)
    for d in range(n_col - 1, 0, -1):
        block = (col + d) % n_col
        in_copy(block).wait_recv()
        at = 0
        for n, part in enumerate(results):
            count = part.shape[0]
            got = landed[block, pl.ds(at, count), :]
            results[n] = part + got.astype(jnp.float32)
            at += count
    for n in range(main // LANES):
        head_grad_ref[:, pl.ds(n * LANES, LANES)] = results[n]
    if tail:
        for j in range(groups):
            here = results[-1]
            if j > 0:
                here = pltpu.roll(here, LANES - j * tail, 1)
            head_grad_ref[pl.ds(j * tail_rows, tail_rows), pl.ds(main, tail)] = here[:, :tail]

    behind_copy.wait_send()
    back_copy.wait_send()
    for copy in pool_copies:
        copy.wait_send()
    for name in sorted(image_copies):
        image_copies[name].wait_send()
    for d in range(1, n_col):
        in_copy((col + d) % n_col).wait_send()


def deliver(text_grad, head_grad):
    def move(text_from, head_from, text_to, head_to, sems):
        copies = [
            pltpu.make_async_copy(text_from, text_to, sems.at[0]),
            pltpu.make_async_copy(head_from, head_to, sems.at[1]),
        ]
        for copy in copies:
            copy.start()
        for copy in copies:
            copy.wait()

    vmem = pl.BlockSpec(memory_space=pltpu.VMEM)
    anywhere = pl.BlockSpec(memory_space=pl.ANY)
    return pl.pallas_call(
        move,
        out_shape=(
            jax.ShapeDtypeStruct(text_grad.shape, text_grad.dtype),
            jax.ShapeDtypeStruct(head_grad.shape, head_grad.dtype),
        ),
        in_specs=[vmem, vmem],
        out_specs=(anywhere, anywhere),
        scratch_shapes=[pltpu.SemaphoreType.DMA((2,))],
    )(
        pltpu.with_memory_space_constraint(text_grad, pltpu.VMEM),
        pltpu.with_memory_space_constraint(head_grad, pltpu.VMEM),
    )


def plan_of(width, n_row, n_col):
    head_rows, head_cols = width // n_row, width // n_col
    chunks = next((n for n in (3, 2, 1) if width % (n * LANES) == 0), None)
    spans = [aligned(c * head_cols, (c + 1) * head_cols) for c in range(n_col)]
    window = max(stop - start for start, stop in spans)
    starts = [start for start, _ in spans]
    if chunks is None or any(start + window > width for start in starts):
        return None
    ready = [
        max(starts[c] + window, width - starts[n_col - 1 - c]) for c in range(n_col)
    ]
    tail = head_cols % LANES
    fitting = [
        n
        for n in range(1, LANES // tail + 1 if tail else 2)
        if head_rows % (16 * n) == 0
    ]
    if not fitting or head_cols < LANES:
        return None
    return chunks, ready, window, head_rows // max(fitting)


def fused_body(n_row, n_col, pooled, text_embed, head_weight, logit_scale, logit_bias, partner):
    rows, width = pooled.shape
    factor = 1.0 / math.sqrt(rows * n_row * n_col)
    chunks, ready, window, tail_rows = plan_of(width, n_row, n_col)
    head_cols = width // n_col
    packed_rows = head_cols // LANES * (width // n_row)
    packed_rows += tail_rows if head_cols % LANES else 0
    bounds = [0, width // 8, width // 4, width // 2, width]
    spans = [aligned(bounds[q], bounds[q + 1]) for q in range(4)]
    masked_width = sum(stop - start for start, stop in spans)
    head_rows, head_cols = width // n_row, width // n_col
    vmem = pl.BlockSpec(memory_space=pltpu.VMEM)
    dma = pltpu.SemaphoreType.DMA
    return pl.pallas_call(
        functools.partial(
            kernel, n_row, n_col, factor, chunks, ready, window, tail_rows
        ),
        out_shape=(
            pltpu.VMEM((rows, width), jnp.float32),
            pltpu.VMEM((head_rows, head_cols), jnp.float32),
        ),
        in_specs=[pl.BlockSpec(memory_space=pl.ANY)] * 6,
        out_specs=(vmem, vmem),
        scratch_shapes=[
            pltpu.VMEM(pooled.shape, jnp.bfloat16),
            pltpu.VMEM(text_embed.shape, jnp.bfloat16),
            pltpu.VMEM(head_weight.shape, jnp.bfloat16),
            pltpu.SMEM(logit_scale.shape, jnp.float32),
            pltpu.SMEM(logit_bias.shape, jnp.float32),
            pltpu.VMEM(partner.shape, jnp.int32),
            dma((6,)),
            pltpu.VMEM((rows, width), jnp.float32),
            pltpu.VMEM((rows, width), jnp.bfloat16),
            pltpu.VMEM((rows, width), jnp.bfloat16),
            pltpu.VMEM((rows, width), jnp.bfloat16),
            pltpu.VMEM((width, rows), jnp.bfloat16),
            pltpu.VMEM((head_rows, n_row * rows), jnp.bfloat16),
            pltpu.VMEM((rows, width), jnp.bfloat16),
            pltpu.VMEM((rows, masked_width), jnp.bfloat16),
            pltpu.VMEM((n_row * rows, width), jnp.bfloat16),
            pltpu.VMEM((head_rows, width), jnp.float32),
            pltpu.VMEM((n_col, packed_rows, LANES), jnp.bfloat16),
            pltpu.VMEM((n_col, packed_rows, LANES), jnp.bfloat16),
            dma((2,)),
            dma((2,)),
            dma((n_row,)),
            dma((n_row,)),
            dma((n_row + 1, chunks)),
            dma((n_row + 1, chunks)),
            dma((n_col,)),
            dma((n_col,)),
        ],
        compiler_params=pltpu.CompilerParams(collective_id=0, has_side_effects=True),
    )(pooled, text_embed, head_weight, logit_scale, logit_bias, partner)


def per_device(n_row, n_col):
    def run(pooled, text_embed, head_weight, logit_scale, logit_bias, partner):
        rows, width = pooled.shape
        fused = (
            n_row == 2**3
            and n_col > 1
            and rows == LANES
            and width % LANES == 0
            and width % (16 * n_row) == 0
            and width % n_col == 0
            and plan_of(width, n_row, n_col) is not None
        )
        args = (pooled, text_embed, head_weight, logit_scale, logit_bias, partner)
        return deliver(*fused_body(n_row, n_col, *args)) if fused else body(*args)

    return run


def solution(mesh):
    in_specs = (
        P(("row", "col"), None),
        P(("row", "col"), None),
        P(),
        P(),
        P(),
        P(("row", "col"), None),
    )
    out_specs = (P(("row", "col"), None), P("row", "col"))
    run = per_device(mesh.shape["row"], mesh.shape["col"])
    return jax.shard_map(run, mesh=mesh, in_specs=in_specs, out_specs=out_specs, check_vma=False)
```

```python
import functools
import math

import jax
import jax.numpy as jnp
from jax import lax
from jax.experimental import pallas as pl
from jax.experimental.pallas import tpu as pltpu
from jax.sharding import PartitionSpec as P

LANES = 128
MESH = pl.DeviceIdType.MESH


def shifted(value, axis, by):
    count = lax.axis_size(axis)
    return lax.ppermute(value, axis, [(i, (i + by) % count) for i in range(count)])


def segment_weights(image_part, text_part, positive, logit_scale, logit_bias, factor):
    model_width = image_part.shape[1]
    bounds = [0, model_width // 8, model_width // 4, model_width // 2, model_width]
    running = jnp.zeros((image_part.shape[0], text_part.shape[0]), jnp.float32)
    level_grads = []
    for prefix in range(4):
        low_end = bounds[prefix]
        high_end = bounds[prefix + 1]
        running = running + jnp.dot(
            image_part[:, low_end:high_end],
            text_part[:, low_end:high_end].T,
            preferred_element_type=jnp.float32,
        )
        logits = logit_scale[prefix] * running + logit_bias[prefix]
        level_grads.append((jax.nn.sigmoid(logits) - positive) * factor)
    weights = []
    carried = jnp.zeros_like(running)
    for prefix in range(3, -1, -1):
        carried = carried + logit_scale[prefix] * level_grads[prefix]
        weights.insert(0, carried.astype(jnp.bfloat16))
    return (weights, bounds)


def image_side(weights, bounds, text_part):
    pieces = []
    for prefix in range(4):
        pieces.append(
            jnp.dot(
                weights[prefix],
                text_part[:, bounds[prefix] : bounds[prefix + 1]],
                preferred_element_type=jnp.float32,
            )
        )
    return jnp.concatenate(pieces, 1)


def text_side(weights, bounds, image_part):
    pieces = []
    for prefix in range(4):
        pieces.append(
            jnp.dot(
                weights[prefix].T,
                image_part[:, bounds[prefix] : bounds[prefix + 1]],
                preferred_element_type=jnp.float32,
            )
        )
    return jnp.concatenate(pieces, 1)


def body(pooled, text_embed, head_weight, logit_scale, logit_bias, partner):
    block_rows = pooled.shape[0]
    factor = 1.0 / math.sqrt(block_rows * lax.axis_size("row") * lax.axis_size("col"))
    embedding = jnp.dot(pooled, head_weight, preferred_element_type=jnp.float32).astype(
        jnp.bfloat16
    )
    local_ids = jnp.arange(block_rows, dtype=jnp.int32)
    positive = (partner[0][:, None] == local_ids[None, :]).astype(jnp.float32)
    empty = jnp.zeros((block_rows, block_rows), jnp.float32)
    weights, bounds = segment_weights(
        embedding, text_embed, positive, logit_scale, logit_bias, factor
    )
    own_image = image_side(weights, bounds, text_embed)
    own_text = text_side(weights, bounds, embedding)
    behind = shifted(text_embed, "row", 1)
    weights, bounds = segment_weights(embedding, behind, empty, logit_scale, logit_bias, factor)
    cross_image = image_side(weights, bounds, behind)
    cross_text = text_side(weights, bounds, embedding)
    returned = shifted(cross_text.astype(jnp.bfloat16), "row", -1).astype(cross_text.dtype)
    text_grad = own_text + returned
    image_grad = own_image + cross_image
    column_block = lax.all_to_all(
        image_grad.astype(jnp.bfloat16), "col", split_axis=1, concat_axis=0, tiled=True
    ).astype(image_grad.dtype)
    group_rows = lax.all_gather(pooled, "col", axis=0, tiled=True)
    block_term = jnp.dot(
        group_rows.astype(jnp.float32).T, column_block, precision=lax.Precision.HIGHEST
    )
    head_grad = lax.psum_scatter(block_term, "row", scatter_dimension=0, tiled=True)
    return (text_grad, head_grad)


def dot_nt(left, right):
    return lax.dot_general(
        left, right, (((1,), (1,)), ((), ())), preferred_element_type=jnp.float32
    )


def dot_nn(left, right):
    return jnp.dot(left, right, preferred_element_type=jnp.float32)


def aligned(low_end, high_end):
    return low_end // LANES * LANES, -(-high_end // LANES) * LANES


def weights_of(score_of, positive, scale_ref, bias_ref, factor):
    running = None
    level_grads = []
    for prefix in range(4):
        part = score_of(prefix)
        running = part if running is None else running + part
        gate = jax.nn.sigmoid(scale_ref[prefix] * running + bias_ref[prefix])
        if positive is not None:
            gate = gate - positive
        level_grads.append(gate * factor)
    weights = [None] * 4
    carried = None
    for prefix in range(3, -1, -1):
        term = scale_ref[prefix] * level_grads[prefix]
        carried = term if carried is None else carried + term
        weights[prefix] = carried.astype(jnp.bfloat16)
    return weights


def by_tile(piece_of, bounds, store):
    pieces = []
    for q in range(4):
        start, stop = aligned(bounds[q], bounds[q + 1])
        pieces.append((start, stop, piece_of(q, start, stop)))
    for tile in range(bounds[4] // LANES):
        base = tile * LANES
        value = None
        for q in range(4):
            start, stop, piece = pieces[q]
            if start <= base < stop:
                here = piece[:, base - start : base - start + LANES]
                if value is None:
                    value = here
                else:
                    lane = lax.broadcasted_iota(jnp.int32, here.shape, 1)
                    value = jnp.where(lane < bounds[q] - base, value, here)
        store(base, value)


def kernel(
    n_row,
    n_col,
    factor,
    plan,
    pooled_hbm,
    text_hbm,
    weight_hbm,
    scale_hbm,
    bias_hbm,
    partner_hbm,
    text_grad_ref,
    head_grad_ref,
    pooled_ref,
    text_ref,
    weight_ref,
    scale_ref,
    bias_ref,
    partner_ref,
    load_sem,
    image_sum,
    cross_text,
    text_back,
    text_behind,
    pooled_t,
    pooled_in,
    embed,
    masked,
    image_out,
    image_in,
    total,
    x_out,
    x_in,
    z_out,
    z_in,
    near_send,
    near_recv,
    pool_send,
    pool_recv,
    image_send,
    image_recv,
    x_send,
    x_recv,
    z_send,
    z_recv,
):
    window, image_tail, out_tail = plan
    rows, width = pooled_hbm.shape
    head_rows = width // n_row
    head_cols = width // n_col
    tiles = head_cols // LANES
    tail = head_cols % LANES
    bounds = [0, width // 8, width // 4, width // 2, width]
    row = lax.axis_index("row")
    col = lax.axis_index("col")
    half = n_row // 2
    y = row // half
    x = row // 2 % 2
    core = row % 2
    pair = col % 2
    side = col // 2

    other_core = row + 1 - 2 * core
    over_y = (row + half) % n_row
    over_y_other = over_y + 1 - 2 * core
    over_x = row + 2 - 4 * x
    over_z = col + 1 - 2 * pair
    far_z = (col + 2) % n_col

    barrier = pltpu.get_barrier_semaphore()
    peers = (
        ((row + 1) % n_row, col),
        ((row + n_row - 1) % n_row, col),
        (over_x, col),
        (over_y, col),
        (over_y_other, col),
        (row, over_z),
        (other_core, over_z),
        (row, far_z),
    )
    for peer in peers:
        pl.semaphore_signal(barrier, inc=1, device_id=peer, device_id_type=MESH)

    loads = [
        pltpu.make_async_copy(src, dst, load_sem.at[n])
        for n, (src, dst) in enumerate(
            (
                (pooled_hbm, pooled_ref),
                (weight_hbm, weight_ref),
                (text_hbm, text_ref),
                (scale_hbm, scale_ref),
                (bias_hbm, bias_ref),
                (partner_hbm, partner_ref),
            )
        )
    ]
    for load in loads:
        load.start()

    def remote(src, dst, send, recv, device):
        return pltpu.make_async_remote_copy(
            src_ref=src,
            dst_ref=dst,
            send_sem=send,
            recv_sem=recv,
            device_id=device,
            device_id_type=MESH,
        )

    behind_copy = remote(
        text_hbm, text_behind, near_send.at[0], near_recv.at[0], ((row + 1) % n_row, col)
    )
    back_copy = remote(
        cross_text,
        text_back,
        near_send.at[1],
        near_recv.at[1],
        ((row + n_row - 1) % n_row, col),
    )
    pl.semaphore_wait(barrier, len(peers))
    behind_copy.start()
    loads[0].wait()

    for tile in range(width // LANES):
        part = pooled_ref[:, pl.ds(tile * LANES, LANES)].T
        at = tile * LANES
        while at < (tile + 1) * LANES:
            block = at // head_rows
            stop = min((block + 1) * head_rows, (tile + 1) * LANES)
            pooled_t[block // 2, block % 2, pl.ds(at - block * head_rows, stop - at), :] = part[
                at - tile * LANES : stop - tile * LANES
            ]
            at = stop

    def pool_copy(src, slot, device):
        return remote(src, pooled_in.at[slot], pool_send.at[slot], pool_recv.at[slot], device)

    def pooled_for(half_y, half_core):
        return pooled_t.at[pl.ds(2 * half_y, 2), half_core]

    pool_copies = {
        4: pool_copy(pooled_for(y, core), 4, (row, over_z)),
        5: pool_copy(pooled_for(y, 1 - core), 5, (other_core, over_z)),
        2: pool_copy(pooled_for(1 - y, core), 2, (over_y, col)),
        3: pool_copy(pooled_for(1 - y, 1 - core), 3, (over_y_other, col)),
        1: pool_copy(pooled_for(y, 1 - core), 1, (other_core, col)),
    }
    for copy in pool_copies.values():
        copy.start()
    for slot in (6, 7):
        pool_copies[slot] = pool_copy(pooled_in.at[slot - 4], slot, (row, over_z))
    pooled_in[0] = pooled_t[pl.ds(2 * y, 2), core]

    def fill_embed(source):
        at = 0
        for q in range(4):
            start, stop = aligned(bounds[q], bounds[q + 1])
            at += stop - start
        step = 3 * LANES if width % (3 * LANES) == 0 else LANES
        for base in range(0, width, step):
            part = dot_nn(source[...], weight_ref[:, pl.ds(base, step)])
            embed[:, pl.ds(base, step)] = part.astype(jnp.bfloat16)
        at = 0
        for q in range(4):
            start, stop = aligned(bounds[q], bounds[q + 1])
            part = embed[:, pl.ds(start, stop - start)].astype(jnp.float32)
            lane = lax.broadcasted_iota(jnp.int32, part.shape, 1) + start
            keep = (lane >= bounds[q]) & (lane < bounds[q + 1])
            masked[:, pl.ds(at, stop - start)] = jnp.where(keep, part, 0.0).astype(
                jnp.bfloat16
            )
            at += stop - start

    def masked_part(q):
        at = 0
        for before in range(q):
            start, stop = aligned(bounds[before], bounds[before + 1])
            at += stop - start
        start, stop = aligned(bounds[q], bounds[q + 1])
        return masked[:, pl.ds(at, stop - start)]

    def text_part(ref, q):
        start, stop = aligned(bounds[q], bounds[q + 1])
        return ref[:, pl.ds(start, stop - start)]

    loads[1].wait()
    fill_embed(pooled_ref)
    for load in loads[2:]:
        load.wait()
    text_id = lax.broadcasted_iota(jnp.int32, (rows, rows), 0)
    positive = (text_id == partner_ref[...]).astype(jnp.float32).T
    own = weights_of(
        lambda q: dot_nt(masked_part(q), text_part(text_ref, q)),
        positive,
        scale_ref,
        bias_ref,
        factor,
    )

    def own_image_piece(q, start, stop):
        return dot_nn(own[q], text_ref[:, pl.ds(start, stop - start)])

    def keep_image(base, value):
        image_sum[:, pl.ds(base, LANES)] = value

    by_tile(own_image_piece, bounds, keep_image)

    def folded(value, kept):
        lane = lax.broadcasted_iota(jnp.int32, value.shape, 1)
        value = jnp.where(lane < tail, value, 0.0)
        joined = value[:kept]
        for n in range(1, value.shape[0] // kept):
            joined = joined + pltpu.roll(value[n * kept : (n + 1) * kept], n * tail, 1)
        return joined

    def block_of(turn, parity):
        return parity + 2 * (side if turn == 1 else 1 - side)

    def image_copy(src, slot, turn, device):
        return remote(
            src,
            image_in.at[turn, slot],
            image_send.at[slot, turn],
            image_recv.at[slot, turn],
            device,
        )

    image_copies = {}
    for turn in range(2):
        mine = image_out.at[block_of(turn, pair)]
        theirs = image_out.at[block_of(turn, 1 - pair)]
        held = [image_in.at[turn, slot] for slot in range(8)]
        image_copies[4, turn] = image_copy(theirs, 4, turn, (row, over_z))
        image_copies[2, turn] = image_copy(mine, 2, turn, (over_y, col))
        image_copies[1, turn] = image_copy(mine, 1, turn, (other_core, col))
        image_copies[6, turn] = image_copy(held[4], 6, turn, (over_y, col))
        for slot in (3, 5, 7):
            image_copies[slot, turn] = image_copy(held[slot - 1], slot, turn, (other_core, col))

    def cross_phase():
        behind_copy.wait_recv()
        cross = weights_of(
            lambda q: dot_nt(masked_part(q), text_part(text_behind, q)),
            None,
            scale_ref,
            bias_ref,
            factor,
        )

        def image_piece(q, start, stop):
            return dot_nn(cross[q], text_behind[:, pl.ds(start, stop - start)])

        def add_image(base, value):
            lanes = pl.ds(base, LANES)
            image_sum[:, lanes] = image_sum[:, lanes] + value

        by_tile(image_piece, bounds, add_image)
        for block in range(n_col):
            first = block * head_cols // LANES * LANES
            offset = block * head_cols - first
            part = image_sum[:, pl.ds(first, window)]
            if offset:
                part = pltpu.roll(part, window - offset, 1)
            for n in range(tiles):
                image_out[block, pl.ds(n * rows, rows), :] = part[
                    :, n * LANES : (n + 1) * LANES
                ].astype(jnp.bfloat16)
            if tail:
                last = folded(part[:, tiles * LANES : (tiles + 1) * LANES], image_tail)
                image_out[block, pl.ds(tiles * rows, image_tail), :] = last.astype(jnp.bfloat16)
        for turn in range(2):
            for slot in (4, 2, 1):
                image_copies[slot, turn].start()

        def own_text_piece(q, start, stop):
            return dot_nn(own[q].T, embed[:, pl.ds(start, stop - start)])

        def store_text(base, value):
            text_grad_ref[:, pl.ds(base, LANES)] = value

        def cross_text_piece(q, start, stop):
            return dot_nn(cross[q].T, embed[:, pl.ds(start, stop - start)])

        def store_cross(base, value):
            cross_text[:, pl.ds(base, LANES)] = value.astype(jnp.bfloat16)

        by_tile(cross_text_piece, bounds, store_cross)
        back_copy.start()
        by_tile(own_text_piece, bounds, store_text)

    pl.when(core == 1)(cross_phase)
    for slot in (6, 7):
        pool_copies[slot - 4].wait_recv()
        pool_copies[slot].start()
    pl.when(core == 0)(cross_phase)

    for turn in range(2):
        image_in[turn, 0] = image_out[block_of(turn, pair)]

    def forward(slot, turn):
        image_copies[slot, turn].wait_recv()
        if slot == 4:
            image_copies[6, turn].start()
        image_copies[slot + 1, turn].start()

    for turn in range(2):
        forward(4, turn)
        forward(2, turn)
    forward(6, 0)
    for slot in (1, 4, 5, 6, 7):
        pool_copies[slot].wait_recv()

    parts = [(n * head_rows, head_rows) for n in range(tiles)]
    if tail:
        parts.append((tiles * head_rows, out_tail))

    def part_of(ref, n):
        return ref.at[pl.ds(parts[n][0], parts[n][1]), :]

    x_copies = {
        (turn, n): remote(
            part_of(x_out.at[turn], n),
            part_of(x_in.at[turn], n),
            x_send.at[turn, n],
            x_recv.at[turn, n],
            (over_x, col),
        )
        for turn in range(2)
        for n in range(len(parts))
    }
    z_copies = [
        remote(part_of(z_out, n), part_of(z_in, n), z_send.at[n], z_recv.at[n], (row, far_z))
        for n in range(len(parts))
    ]

    def keep_part(turn, n, value):
        first, count = parts[n]
        for there in range(2):
            piece = value[there * head_rows : (there + 1) * head_rows]
            if n == tiles:
                piece = folded(piece, count)
            total[turn, there, pl.ds(first, count), :] = piece
        x_out[turn, pl.ds(first, count), :] = total[
            turn, 1 - x, pl.ds(first, count), :
        ].astype(jnp.bfloat16)
        x_copies[turn, n].start()

    def multiply(turn):
        for slot in (1, 3, 5, 7):
            image_copies[slot, turn].wait_recv()
        left = jnp.concatenate(
            [pooled_in[slot].reshape(2 * head_rows, rows) for slot in range(8)], 1
        )
        sides = [
            image_in[turn, :, pl.ds(n * rows, rows), :].reshape(8 * rows, LANES)
            for n in range(tiles)
        ]
        main = dot_nn(left, jnp.concatenate(sides, 1))
        for n in range(tiles):
            keep_part(turn, n, main[:, n * LANES : (n + 1) * LANES])
        if tail:
            pieces = []
            for slot in range(8):
                held = image_in[turn, slot, pl.ds(tiles * rows, image_tail), :]
                held = held.astype(jnp.float32)
                for n in range(rows // image_tail):
                    moved = pltpu.roll(held, LANES - n * tail, 1) if n else held
                    pieces.append(moved.astype(jnp.bfloat16))
            keep_part(turn, tiles, dot_nn(left, jnp.concatenate(pieces, 0)))

    @pl.when(core == 1)
    def _():
        forward(6, 1)

    multiply(0)

    @pl.when(core == 0)
    def _():
        forward(6, 1)

    multiply(1)
    for n, (first, count) in enumerate(parts):
        at = pl.ds(first, count)
        x_copies[0, n].wait_recv()
        value = total[0, x, at, :] + x_in[0, at, :].astype(jnp.float32)
        z_out[at, :] = value.astype(jnp.bfloat16)
        z_copies[n].start()

    back_copy.wait_recv()
    text_grad_ref[...] = text_grad_ref[...] + text_back[...].astype(jnp.float32)

    for n, (first, count) in enumerate(parts):
        at = pl.ds(first, count)
        x_copies[1, n].wait_recv()
        value = total[1, x, at, :] + x_in[1, at, :].astype(jnp.float32)
        z_copies[n].wait_recv()
        value = value + z_in[at, :].astype(jnp.float32)
        if n < tiles:
            head_grad_ref[:, pl.ds(n * LANES, LANES)] = value
        else:
            for j in range(head_rows // count):
                here = pltpu.roll(value, LANES - j * tail, 1) if j else value
                head_grad_ref[pl.ds(j * count, count), pl.ds(tiles * LANES, tail)] = here[:, :tail]

    behind_copy.wait_send()
    back_copy.wait_send()
    for copies in (pool_copies, image_copies, x_copies):
        for name in sorted(copies):
            copies[name].wait_send()
    for copy in z_copies:
        copy.wait_send()


def deliver(text_grad, head_grad):
    def move(text_from, head_from, text_to, head_to, sems):
        copies = [
            pltpu.make_async_copy(text_from, text_to, sems.at[0]),
            pltpu.make_async_copy(head_from, head_to, sems.at[1]),
        ]
        for copy in copies:
            copy.start()
        for copy in copies:
            copy.wait()

    vmem = pl.BlockSpec(memory_space=pltpu.VMEM)
    anywhere = pl.BlockSpec(memory_space=pl.ANY)
    return pl.pallas_call(
        move,
        out_shape=(
            jax.ShapeDtypeStruct(text_grad.shape, text_grad.dtype),
            jax.ShapeDtypeStruct(head_grad.shape, head_grad.dtype),
        ),
        in_specs=[vmem, vmem],
        out_specs=(anywhere, anywhere),
        scratch_shapes=[pltpu.SemaphoreType.DMA((2,))],
    )(
        pltpu.with_memory_space_constraint(text_grad, pltpu.VMEM),
        pltpu.with_memory_space_constraint(head_grad, pltpu.VMEM),
    )


def fold_of(count, tail):
    fitting = [n for n in range(1, LANES // tail + 1 if tail else 2) if count % (16 * n) == 0]
    return count // max(fitting) if fitting else None


def plan_of(rows, width, n_row, n_col):
    head_rows, head_cols = width // n_row, width // n_col
    spans = [aligned(c * head_cols, (c + 1) * head_cols) for c in range(n_col)]
    window = max(stop - start for start, stop in spans)
    if head_cols < LANES or any(start + window > width for start, _ in spans):
        return None
    image_tail = fold_of(rows, head_cols % LANES)
    out_tail = fold_of(head_rows, head_cols % LANES)
    if image_tail is None or out_tail is None:
        return None
    return window, image_tail, out_tail


def fused_body(n_row, n_col, pooled, text_embed, head_weight, logit_scale, logit_bias, partner):
    rows, width = pooled.shape
    factor = 1.0 / math.sqrt(rows * n_row * n_col)
    plan = plan_of(rows, width, n_row, n_col)
    _, image_tail, out_tail = plan
    head_rows, head_cols = width // n_row, width // n_col
    tiles, ragged = head_cols // LANES, head_cols % LANES > 0
    image_rows = tiles * rows + ragged * image_tail
    out_rows = tiles * head_rows + ragged * out_tail
    parts = tiles + ragged
    bounds = [0, width // 8, width // 4, width // 2, width]
    spans = [aligned(bounds[q], bounds[q + 1]) for q in range(4)]
    masked_width = sum(stop - start for start, stop in spans)
    vmem = pl.BlockSpec(memory_space=pltpu.VMEM)
    dma = pltpu.SemaphoreType.DMA
    bf16, f32 = jnp.bfloat16, jnp.float32
    return pl.pallas_call(
        functools.partial(kernel, n_row, n_col, factor, plan),
        out_shape=(
            pltpu.VMEM((rows, width), jnp.float32),
            pltpu.VMEM((head_rows, head_cols), jnp.float32),
        ),
        in_specs=[pl.BlockSpec(memory_space=pl.ANY)] * 6,
        out_specs=(vmem, vmem),
        scratch_shapes=[
            pltpu.VMEM(pooled.shape, bf16),
            pltpu.VMEM(text_embed.shape, bf16),
            pltpu.VMEM(head_weight.shape, bf16),
            pltpu.SMEM(logit_scale.shape, f32),
            pltpu.SMEM(logit_bias.shape, f32),
            pltpu.VMEM(partner.shape, jnp.int32),
            dma((6,)),
            pltpu.VMEM((rows, width), f32),
            pltpu.VMEM((rows, width), bf16),
            pltpu.VMEM((rows, width), bf16),
            pltpu.VMEM((rows, width), bf16),
            pltpu.VMEM((n_row // 2, 2, head_rows, rows), bf16),
            pltpu.VMEM((8, 2, head_rows, rows), bf16),
            pltpu.VMEM((rows, width), bf16),
            pltpu.VMEM((rows, masked_width), bf16),
            pltpu.VMEM((n_col, image_rows, LANES), bf16),
            pltpu.VMEM((2, 8, image_rows, LANES), bf16),
            pltpu.VMEM((2, 2, out_rows, LANES), f32),
            pltpu.VMEM((2, out_rows, LANES), bf16),
            pltpu.VMEM((2, out_rows, LANES), bf16),
            pltpu.VMEM((out_rows, LANES), bf16),
            pltpu.VMEM((out_rows, LANES), bf16),
            dma((2,)),
            dma((2,)),
            dma((8,)),
            dma((8,)),
            dma((8, 2)),
            dma((8, 2)),
            dma((2, parts)),
            dma((2, parts)),
            dma((parts,)),
            dma((parts,)),
        ],
        compiler_params=pltpu.CompilerParams(collective_id=0, has_side_effects=True),
    )(pooled, text_embed, head_weight, logit_scale, logit_bias, partner)


def per_device(n_row, n_col):
    def run(pooled, text_embed, head_weight, logit_scale, logit_bias, partner):
        rows, width = pooled.shape
        fused = (
            n_row == 2**3
            and n_col == 2**2
            and rows == LANES
            and width % LANES == 0
            and width % (16 * n_row) == 0
            and width % n_col == 0
            and plan_of(rows, width, n_row, n_col) is not None
        )
        args = (pooled, text_embed, head_weight, logit_scale, logit_bias, partner)
        return deliver(*fused_body(n_row, n_col, *args)) if fused else body(*args)

    return run


def solution(mesh):
    in_specs = (
        P(("row", "col"), None),
        P(("row", "col"), None),
        P(),
        P(),
        P(),
        P(("row", "col"), None),
    )
    out_specs = (P(("row", "col"), None), P("row", "col"))
    run = per_device(mesh.shape["row"], mesh.shape["col"])
    return jax.shard_map(run, mesh=mesh, in_specs=in_specs, out_specs=out_specs, check_vma=False)
```

```python
import functools
import math

import jax
import jax.numpy as jnp
from jax import lax
from jax.experimental import pallas as pl
from jax.experimental.pallas import tpu as pltpu
from jax.sharding import PartitionSpec as P

LANES = 128
MESH = pl.DeviceIdType.MESH


def shifted(value, axis, by):
    count = lax.axis_size(axis)
    return lax.ppermute(value, axis, [(i, (i + by) % count) for i in range(count)])


def segment_weights(image_part, text_part, positive, logit_scale, logit_bias, factor):
    model_width = image_part.shape[1]
    bounds = [0, model_width // 8, model_width // 4, model_width // 2, model_width]
    running = jnp.zeros((image_part.shape[0], text_part.shape[0]), jnp.float32)
    level_grads = []
    for prefix in range(4):
        low_end = bounds[prefix]
        high_end = bounds[prefix + 1]
        running = running + jnp.dot(
            image_part[:, low_end:high_end],
            text_part[:, low_end:high_end].T,
            preferred_element_type=jnp.float32,
        )
        logits = logit_scale[prefix] * running + logit_bias[prefix]
        level_grads.append((jax.nn.sigmoid(logits) - positive) * factor)
    weights = []
    carried = jnp.zeros_like(running)
    for prefix in range(3, -1, -1):
        carried = carried + logit_scale[prefix] * level_grads[prefix]
        weights.insert(0, carried.astype(jnp.bfloat16))
    return (weights, bounds)


def image_side(weights, bounds, text_part):
    pieces = []
    for prefix in range(4):
        pieces.append(
            jnp.dot(
                weights[prefix],
                text_part[:, bounds[prefix] : bounds[prefix + 1]],
                preferred_element_type=jnp.float32,
            )
        )
    return jnp.concatenate(pieces, 1)


def text_side(weights, bounds, image_part):
    pieces = []
    for prefix in range(4):
        pieces.append(
            jnp.dot(
                weights[prefix].T,
                image_part[:, bounds[prefix] : bounds[prefix + 1]],
                preferred_element_type=jnp.float32,
            )
        )
    return jnp.concatenate(pieces, 1)


def body(pooled, text_embed, head_weight, logit_scale, logit_bias, partner):
    block_rows = pooled.shape[0]
    factor = 1.0 / math.sqrt(block_rows * lax.axis_size("row") * lax.axis_size("col"))
    embedding = jnp.dot(pooled, head_weight, preferred_element_type=jnp.float32).astype(
        jnp.bfloat16
    )
    local_ids = jnp.arange(block_rows, dtype=jnp.int32)
    positive = (partner[0][:, None] == local_ids[None, :]).astype(jnp.float32)
    empty = jnp.zeros((block_rows, block_rows), jnp.float32)
    weights, bounds = segment_weights(
        embedding, text_embed, positive, logit_scale, logit_bias, factor
    )
    own_image = image_side(weights, bounds, text_embed)
    own_text = text_side(weights, bounds, embedding)
    behind = shifted(text_embed, "row", 1)
    weights, bounds = segment_weights(embedding, behind, empty, logit_scale, logit_bias, factor)
    cross_image = image_side(weights, bounds, behind)
    cross_text = text_side(weights, bounds, embedding)
    returned = shifted(cross_text.astype(jnp.bfloat16), "row", -1).astype(cross_text.dtype)
    text_grad = own_text + returned
    image_grad = own_image + cross_image
    column_block = lax.all_to_all(
        image_grad.astype(jnp.bfloat16), "col", split_axis=1, concat_axis=0, tiled=True
    ).astype(image_grad.dtype)
    group_rows = lax.all_gather(pooled, "col", axis=0, tiled=True)
    block_term = jnp.dot(
        group_rows.astype(jnp.float32).T, column_block, precision=lax.Precision.HIGHEST
    )
    head_grad = lax.psum_scatter(block_term, "row", scatter_dimension=0, tiled=True)
    return (text_grad, head_grad)


def dot_nt(left, right):
    return lax.dot_general(
        left, right, (((1,), (1,)), ((), ())), preferred_element_type=jnp.float32
    )


def dot_nn(left, right):
    return jnp.dot(left, right, preferred_element_type=jnp.float32)


def aligned(low_end, high_end):
    return low_end // LANES * LANES, -(-high_end // LANES) * LANES


def weights_of(score_of, positive, scale_ref, bias_ref, factor):
    running = None
    level_grads = []
    for prefix in range(4):
        part = score_of(prefix)
        running = part if running is None else running + part
        gate = jax.nn.sigmoid(scale_ref[prefix] * running + bias_ref[prefix])
        if positive is not None:
            gate = gate - positive
        level_grads.append(gate * factor)
    weights = [None] * 4
    carried = None
    for prefix in range(3, -1, -1):
        term = scale_ref[prefix] * level_grads[prefix]
        carried = term if carried is None else carried + term
        weights[prefix] = carried.astype(jnp.bfloat16)
    return weights


def by_tile(piece_of, bounds, store):
    pieces = []
    for q in range(4):
        start, stop = aligned(bounds[q], bounds[q + 1])
        pieces.append((start, stop, piece_of(q, start, stop)))
    for tile in range(bounds[4] // LANES):
        base = tile * LANES
        value = None
        for q in range(4):
            start, stop, piece = pieces[q]
            if start <= base < stop:
                here = piece[:, base - start : base - start + LANES]
                if value is None:
                    value = here
                else:
                    lane = lax.broadcasted_iota(jnp.int32, here.shape, 1)
                    value = jnp.where(lane < bounds[q] - base, value, here)
        store(base, value)


def kernel(
    n_row,
    n_col,
    factor,
    plan,
    pooled_hbm,
    text_hbm,
    weight_hbm,
    scale_hbm,
    bias_hbm,
    partner_hbm,
    text_grad_ref,
    head_grad_ref,
    pooled_ref,
    text_ref,
    weight_ref,
    scale_ref,
    bias_ref,
    partner_ref,
    load_sem,
    image_sum,
    cross_text,
    text_back,
    text_behind,
    pooled_t,
    pooled_in,
    embed,
    masked,
    image_out,
    image_in,
    total,
    x_out,
    x_in,
    z_out,
    z_in,
    near_send,
    near_recv,
    pool_send,
    pool_recv,
    image_send,
    image_recv,
    x_send,
    x_recv,
    z_send,
    z_recv,
):
    window, image_tail, out_tail = plan
    rows, width = pooled_hbm.shape
    head_rows = width // n_row
    head_cols = width // n_col
    tiles = head_cols // LANES
    tail = head_cols % LANES
    bounds = [0, width // 8, width // 4, width // 2, width]
    row = lax.axis_index("row")
    col = lax.axis_index("col")
    half = n_row // 2
    y = row // half
    x = row // 2 % 2
    core = row % 2
    pair = col % 2
    side = col // 2

    other_core = row + 1 - 2 * core
    over_y = (row + half) % n_row
    over_y_other = over_y + 1 - 2 * core
    over_x = row + 2 - 4 * x
    over_z = col + 1 - 2 * pair
    far_z = (col + 2) % n_col

    barrier = pltpu.get_barrier_semaphore()
    peers = (
        ((row + 1) % n_row, col),
        ((row + n_row - 1) % n_row, col),
        (over_x, col),
        (over_y, col),
        (over_y_other, col),
        (row, over_z),
        (other_core, over_z),
        (over_y, over_z),
        (row, far_z),
    )
    for peer in peers:
        pl.semaphore_signal(barrier, inc=1, device_id=peer, device_id_type=MESH)

    loads = [
        pltpu.make_async_copy(src, dst, load_sem.at[n])
        for n, (src, dst) in enumerate(
            (
                (pooled_hbm, pooled_ref),
                (weight_hbm, weight_ref),
                (text_hbm, text_ref),
                (scale_hbm, scale_ref),
                (bias_hbm, bias_ref),
                (partner_hbm, partner_ref),
            )
        )
    ]
    for load in loads:
        load.start()

    def remote(src, dst, send, recv, device):
        return pltpu.make_async_remote_copy(
            src_ref=src,
            dst_ref=dst,
            send_sem=send,
            recv_sem=recv,
            device_id=device,
            device_id_type=MESH,
        )

    behind_copy = remote(
        text_hbm, text_behind, near_send.at[0], near_recv.at[0], ((row + 1) % n_row, col)
    )
    back_copy = remote(
        cross_text,
        text_back,
        near_send.at[1],
        near_recv.at[1],
        ((row + n_row - 1) % n_row, col),
    )
    pl.semaphore_wait(barrier, len(peers))
    behind_copy.start()
    loads[0].wait()

    for tile in range(width // LANES):
        part = pooled_ref[:, pl.ds(tile * LANES, LANES)].T
        at = tile * LANES
        while at < (tile + 1) * LANES:
            block = at // head_rows
            stop = min((block + 1) * head_rows, (tile + 1) * LANES)
            pooled_t[block // 2, block % 2, pl.ds(at - block * head_rows, stop - at), :] = part[
                at - tile * LANES : stop - tile * LANES
            ]
            at = stop

    def pool_copy(src, slot, device):
        return remote(src, pooled_in.at[slot], pool_send.at[slot], pool_recv.at[slot], device)

    def pooled_for(half_y, half_core):
        return pooled_t.at[pl.ds(2 * half_y, 2), half_core]

    pool_copies = {
        4: pool_copy(pooled_for(y, core), 4, (row, over_z)),
        5: pool_copy(pooled_for(y, 1 - core), 5, (other_core, over_z)),
        2: pool_copy(pooled_for(1 - y, core), 2, (over_y, col)),
        3: pool_copy(pooled_for(1 - y, 1 - core), 3, (over_y_other, col)),
        1: pool_copy(pooled_for(y, 1 - core), 1, (other_core, col)),
    }
    for copy in pool_copies.values():
        copy.start()
    for slot in (6, 7):
        pool_copies[slot] = pool_copy(pooled_in.at[slot - 4], slot, (row, over_z))
    pooled_in[0] = pooled_t[pl.ds(2 * y, 2), core]

    def fill_embed(source):
        at = 0
        for q in range(4):
            start, stop = aligned(bounds[q], bounds[q + 1])
            at += stop - start
        step = 3 * LANES if width % (3 * LANES) == 0 else LANES
        for base in range(0, width, step):
            part = dot_nn(source[...], weight_ref[:, pl.ds(base, step)])
            embed[:, pl.ds(base, step)] = part.astype(jnp.bfloat16)
        at = 0
        for q in range(4):
            start, stop = aligned(bounds[q], bounds[q + 1])
            part = embed[:, pl.ds(start, stop - start)].astype(jnp.float32)
            lane = lax.broadcasted_iota(jnp.int32, part.shape, 1) + start
            keep = (lane >= bounds[q]) & (lane < bounds[q + 1])
            masked[:, pl.ds(at, stop - start)] = jnp.where(keep, part, 0.0).astype(
                jnp.bfloat16
            )
            at += stop - start

    def masked_part(q):
        at = 0
        for before in range(q):
            start, stop = aligned(bounds[before], bounds[before + 1])
            at += stop - start
        start, stop = aligned(bounds[q], bounds[q + 1])
        return masked[:, pl.ds(at, stop - start)]

    def text_part(ref, q):
        start, stop = aligned(bounds[q], bounds[q + 1])
        return ref[:, pl.ds(start, stop - start)]

    loads[1].wait()
    fill_embed(pooled_ref)
    for load in loads[2:]:
        load.wait()
    text_id = lax.broadcasted_iota(jnp.int32, (rows, rows), 0)
    positive = (text_id == partner_ref[...]).astype(jnp.float32).T
    own = weights_of(
        lambda q: dot_nt(masked_part(q), text_part(text_ref, q)),
        positive,
        scale_ref,
        bias_ref,
        factor,
    )

    def own_image_piece(q, start, stop):
        return dot_nn(own[q], text_ref[:, pl.ds(start, stop - start)])

    def keep_image(base, value):
        image_sum[:, pl.ds(base, LANES)] = value

    by_tile(own_image_piece, bounds, keep_image)

    def folded(value, kept):
        lane = lax.broadcasted_iota(jnp.int32, value.shape, 1)
        value = jnp.where(lane < tail, value, 0.0)
        joined = value[:kept]
        for n in range(1, value.shape[0] // kept):
            joined = joined + pltpu.roll(value[n * kept : (n + 1) * kept], n * tail, 1)
        return joined

    def block_of(turn, parity):
        return parity + 2 * (side if turn == 1 else 1 - side)

    def image_copy(src, slot, turn, device):
        return remote(
            src,
            image_in.at[turn, slot],
            image_send.at[slot, turn],
            image_recv.at[slot, turn],
            device,
        )

    image_copies = {}
    for turn in range(2):
        mine = image_out.at[block_of(turn, pair)]
        theirs = image_out.at[block_of(turn, 1 - pair)]
        held = [image_in.at[turn, slot] for slot in range(8)]
        image_copies[4, turn] = image_copy(theirs, 4, turn, (row, over_z))
        image_copies[2, turn] = image_copy(mine, 2, turn, (over_y, col))
        image_copies[1, turn] = image_copy(mine, 1, turn, (other_core, col))
        image_copies[6, turn] = image_copy(theirs, 6, turn, (over_y, over_z))
        for slot in (3, 5, 7):
            image_copies[slot, turn] = image_copy(held[slot - 1], slot, turn, (other_core, col))

    def cross_phase():
        behind_copy.wait_recv()
        cross = weights_of(
            lambda q: dot_nt(masked_part(q), text_part(text_behind, q)),
            None,
            scale_ref,
            bias_ref,
            factor,
        )

        def image_piece(q, start, stop):
            return dot_nn(cross[q], text_behind[:, pl.ds(start, stop - start)])

        def add_image(base, value):
            lanes = pl.ds(base, LANES)
            image_sum[:, lanes] = image_sum[:, lanes] + value

        by_tile(image_piece, bounds, add_image)
        def pack(block):
            first = block * head_cols // LANES * LANES
            offset = block * head_cols - first
            part = image_sum[:, pl.ds(pl.multiple_of(first, LANES), window)]
            part = pltpu.roll(part, (window - offset) % window, 1)
            for n in range(tiles):
                image_out[block, pl.ds(n * rows, rows), :] = part[
                    :, n * LANES : (n + 1) * LANES
                ].astype(jnp.bfloat16)
            if tail:
                last = folded(part[:, tiles * LANES : (tiles + 1) * LANES], image_tail)
                image_out[block, pl.ds(tiles * rows, image_tail), :] = last.astype(jnp.bfloat16)

        for turn in range(2):
            for slot in (4, 2):
                pack(block_of(turn, 1 - pair if slot == 4 else pair))
                if turn == 0:
                    image_copies[slot + 2 if slot == 4 else 1, turn].start()
                    image_copies[slot, turn].start()

        def own_text_piece(q, start, stop):
            return dot_nn(own[q].T, embed[:, pl.ds(start, stop - start)])

        def store_text(base, value):
            text_grad_ref[:, pl.ds(base, LANES)] = value

        def cross_text_piece(q, start, stop):
            return dot_nn(cross[q].T, embed[:, pl.ds(start, stop - start)])

        def store_cross(base, value):
            cross_text[:, pl.ds(base, LANES)] = value.astype(jnp.bfloat16)

        by_tile(cross_text_piece, bounds, store_cross)

        @pl.when(core + x > 0)
        def _():
            back_copy.start()

        by_tile(own_text_piece, bounds, store_text)

    cross_phase()
    for slot in (6, 7):
        pool_copies[slot - 4].wait_recv()
        pool_copies[slot].start()

    def forward(slot, turn):
        image_copies[slot, turn].wait_recv()
        image_copies[slot + 1, turn].start()

    forward(4, 0)
    forward(2, 0)
    for slot in (6, 4, 2, 1):
        image_copies[slot, 1].start()
    for turn in range(2):
        image_in[turn, 0] = image_out[block_of(turn, pair)]
    forward(6, 0)
    for slot in (1, 4, 5, 6, 7):
        pool_copies[slot].wait_recv()

    parts = [(n * head_rows, head_rows) for n in range(tiles)]
    if tail:
        parts.append((tiles * head_rows, out_tail))

    def part_of(ref, n):
        return ref.at[pl.ds(parts[n][0], parts[n][1]), :]

    x_copies = {
        (turn, n): remote(
            part_of(x_out.at[turn], n),
            part_of(x_in.at[turn], n),
            x_send.at[turn, n],
            x_recv.at[turn, n],
            (over_x, col),
        )
        for turn in range(2)
        for n in range(len(parts))
    }
    z_copies = [
        remote(part_of(z_out, n), part_of(z_in, n), z_send.at[n], z_recv.at[n], (row, far_z))
        for n in range(len(parts))
    ]

    def keep_part(turn, n, value):
        first, count = parts[n]
        for there in range(2):
            piece = value[there * head_rows : (there + 1) * head_rows]
            if n == tiles:
                piece = folded(piece, count)
            total[turn, there, pl.ds(first, count), :] = piece
        x_out[turn, pl.ds(first, count), :] = total[
            turn, 1 - x, pl.ds(first, count), :
        ].astype(jnp.bfloat16)
        x_copies[turn, n].start()

    def multiply(turn):
        for slot in (1, 3, 5, 7):
            image_copies[slot, turn].wait_recv()
        left = jnp.concatenate(
            [pooled_in[slot].reshape(2 * head_rows, rows) for slot in range(8)], 1
        )
        sides = [
            image_in[turn, :, pl.ds(n * rows, rows), :].reshape(8 * rows, LANES)
            for n in range(tiles)
        ]
        main = dot_nn(left, jnp.concatenate(sides, 1))
        for n in range(tiles):
            keep_part(turn, n, main[:, n * LANES : (n + 1) * LANES])
        if tail:
            pieces = []
            for slot in range(8):
                held = image_in[turn, slot, pl.ds(tiles * rows, image_tail), :]
                held = held.astype(jnp.float32)
                for n in range(rows // image_tail):
                    moved = pltpu.roll(held, LANES - n * tail, 1) if n else held
                    pieces.append(moved.astype(jnp.bfloat16))
            keep_part(turn, tiles, dot_nn(left, jnp.concatenate(pieces, 0)))

    multiply(0)

    @pl.when(core + x == 0)
    def _():
        back_copy.start()

    for slot in (4, 2, 6):
        forward(slot, 1)
    for n, (first, count) in enumerate(parts):
        at = pl.ds(first, count)
        x_copies[0, n].wait_recv()
        value = total[0, x, at, :] + x_in[0, at, :].astype(jnp.float32)
        z_out[at, :] = value.astype(jnp.bfloat16)
        z_copies[n].start()

    multiply(1)
    back_copy.wait_recv()
    text_grad_ref[...] = text_grad_ref[...] + text_back[...].astype(jnp.float32)

    for n, (first, count) in enumerate(parts):
        at = pl.ds(first, count)
        x_copies[1, n].wait_recv()
        value = total[1, x, at, :] + x_in[1, at, :].astype(jnp.float32)
        z_copies[n].wait_recv()
        value = value + z_in[at, :].astype(jnp.float32)
        if n < tiles:
            head_grad_ref[:, pl.ds(n * LANES, LANES)] = value
        else:
            for j in range(head_rows // count):
                here = pltpu.roll(value, LANES - j * tail, 1) if j else value
                head_grad_ref[pl.ds(j * count, count), pl.ds(tiles * LANES, tail)] = here[:, :tail]

    behind_copy.wait_send()
    back_copy.wait_send()
    for copies in (pool_copies, image_copies, x_copies):
        for name in sorted(copies):
            copies[name].wait_send()
    for copy in z_copies:
        copy.wait_send()


def deliver(text_grad, head_grad):
    def move(text_from, head_from, text_to, head_to, sems):
        copies = [
            pltpu.make_async_copy(text_from, text_to, sems.at[0]),
            pltpu.make_async_copy(head_from, head_to, sems.at[1]),
        ]
        for copy in copies:
            copy.start()
        for copy in copies:
            copy.wait()

    vmem = pl.BlockSpec(memory_space=pltpu.VMEM)
    anywhere = pl.BlockSpec(memory_space=pl.ANY)
    return pl.pallas_call(
        move,
        out_shape=(
            jax.ShapeDtypeStruct(text_grad.shape, text_grad.dtype),
            jax.ShapeDtypeStruct(head_grad.shape, head_grad.dtype),
        ),
        in_specs=[vmem, vmem],
        out_specs=(anywhere, anywhere),
        scratch_shapes=[pltpu.SemaphoreType.DMA((2,))],
    )(
        pltpu.with_memory_space_constraint(text_grad, pltpu.VMEM),
        pltpu.with_memory_space_constraint(head_grad, pltpu.VMEM),
    )


def fold_of(count, tail):
    fitting = [n for n in range(1, LANES // tail + 1 if tail else 2) if count % (16 * n) == 0]
    return count // max(fitting) if fitting else None


def plan_of(rows, width, n_row, n_col):
    head_rows, head_cols = width // n_row, width // n_col
    spans = [aligned(c * head_cols, (c + 1) * head_cols) for c in range(n_col)]
    window = max(stop - start for start, stop in spans)
    if head_cols < LANES or any(start + window > width for start, _ in spans):
        return None
    image_tail = fold_of(rows, head_cols % LANES)
    out_tail = fold_of(head_rows, head_cols % LANES)
    if image_tail is None or out_tail is None:
        return None
    return window, image_tail, out_tail


def fused_body(n_row, n_col, pooled, text_embed, head_weight, logit_scale, logit_bias, partner):
    rows, width = pooled.shape
    factor = 1.0 / math.sqrt(rows * n_row * n_col)
    plan = plan_of(rows, width, n_row, n_col)
    _, image_tail, out_tail = plan
    head_rows, head_cols = width // n_row, width // n_col
    tiles, ragged = head_cols // LANES, head_cols % LANES > 0
    image_rows = tiles * rows + ragged * image_tail
    out_rows = tiles * head_rows + ragged * out_tail
    parts = tiles + ragged
    bounds = [0, width // 8, width // 4, width // 2, width]
    spans = [aligned(bounds[q], bounds[q + 1]) for q in range(4)]
    masked_width = sum(stop - start for start, stop in spans)
    vmem = pl.BlockSpec(memory_space=pltpu.VMEM)
    dma = pltpu.SemaphoreType.DMA
    bf16, f32 = jnp.bfloat16, jnp.float32
    return pl.pallas_call(
        functools.partial(kernel, n_row, n_col, factor, plan),
        out_shape=(
            pltpu.VMEM((rows, width), jnp.float32),
            pltpu.VMEM((head_rows, head_cols), jnp.float32),
        ),
        in_specs=[pl.BlockSpec(memory_space=pl.ANY)] * 6,
        out_specs=(vmem, vmem),
        scratch_shapes=[
            pltpu.VMEM(pooled.shape, bf16),
            pltpu.VMEM(text_embed.shape, bf16),
            pltpu.VMEM(head_weight.shape, bf16),
            pltpu.SMEM(logit_scale.shape, f32),
            pltpu.SMEM(logit_bias.shape, f32),
            pltpu.VMEM(partner.shape, jnp.int32),
            dma((6,)),
            pltpu.VMEM((rows, width), f32),
            pltpu.VMEM((rows, width), bf16),
            pltpu.VMEM((rows, width), bf16),
            pltpu.VMEM((rows, width), bf16),
            pltpu.VMEM((n_row // 2, 2, head_rows, rows), bf16),
            pltpu.VMEM((8, 2, head_rows, rows), bf16),
            pltpu.VMEM((rows, width), bf16),
            pltpu.VMEM((rows, masked_width), bf16),
            pltpu.VMEM((n_col, image_rows, LANES), bf16),
            pltpu.VMEM((2, 8, image_rows, LANES), bf16),
            pltpu.VMEM((2, 2, out_rows, LANES), f32),
            pltpu.VMEM((2, out_rows, LANES), bf16),
            pltpu.VMEM((2, out_rows, LANES), bf16),
            pltpu.VMEM((out_rows, LANES), bf16),
            pltpu.VMEM((out_rows, LANES), bf16),
            dma((2,)),
            dma((2,)),
            dma((8,)),
            dma((8,)),
            dma((8, 2)),
            dma((8, 2)),
            dma((2, parts)),
            dma((2, parts)),
            dma((parts,)),
            dma((parts,)),
        ],
        compiler_params=pltpu.CompilerParams(collective_id=0, has_side_effects=True),
    )(pooled, text_embed, head_weight, logit_scale, logit_bias, partner)


def per_device(n_row, n_col):
    def run(pooled, text_embed, head_weight, logit_scale, logit_bias, partner):
        rows, width = pooled.shape
        fused = (
            n_row == 2**3
            and n_col == 2**2
            and rows == LANES
            and width % LANES == 0
            and width % (16 * n_row) == 0
            and width % n_col == 0
            and plan_of(rows, width, n_row, n_col) is not None
        )
        args = (pooled, text_embed, head_weight, logit_scale, logit_bias, partner)
        return deliver(*fused_body(n_row, n_col, *args)) if fused else body(*args)

    return run


def solution(mesh):
    in_specs = (
        P(("row", "col"), None),
        P(("row", "col"), None),
        P(),
        P(),
        P(),
        P(("row", "col"), None),
    )
    out_specs = (P(("row", "col"), None), P("row", "col"))
    run = per_device(mesh.shape["row"], mesh.shape["col"])
    return jax.shard_map(run, mesh=mesh, in_specs=in_specs, out_specs=out_specs, check_vma=False)
```

```python
import functools
import math

import jax
import jax.numpy as jnp
from jax import lax
from jax.experimental import pallas as pl
from jax.experimental.pallas import tpu as pltpu
from jax.sharding import PartitionSpec as P

LANES = 128
MESH = pl.DeviceIdType.MESH


def shifted(value, axis, by):
    count = lax.axis_size(axis)
    return lax.ppermute(value, axis, [(i, (i + by) % count) for i in range(count)])


def segment_weights(image_part, text_part, positive, logit_scale, logit_bias, factor):
    model_width = image_part.shape[1]
    bounds = [0, model_width // 8, model_width // 4, model_width // 2, model_width]
    running = jnp.zeros((image_part.shape[0], text_part.shape[0]), jnp.float32)
    level_grads = []
    for prefix in range(4):
        low_end = bounds[prefix]
        high_end = bounds[prefix + 1]
        running = running + jnp.dot(
            image_part[:, low_end:high_end],
            text_part[:, low_end:high_end].T,
            preferred_element_type=jnp.float32,
        )
        logits = logit_scale[prefix] * running + logit_bias[prefix]
        level_grads.append((jax.nn.sigmoid(logits) - positive) * factor)
    weights = []
    carried = jnp.zeros_like(running)
    for prefix in range(3, -1, -1):
        carried = carried + logit_scale[prefix] * level_grads[prefix]
        weights.insert(0, carried.astype(jnp.bfloat16))
    return (weights, bounds)


def image_side(weights, bounds, text_part):
    pieces = []
    for prefix in range(4):
        pieces.append(
            jnp.dot(
                weights[prefix],
                text_part[:, bounds[prefix] : bounds[prefix + 1]],
                preferred_element_type=jnp.float32,
            )
        )
    return jnp.concatenate(pieces, 1)


def text_side(weights, bounds, image_part):
    pieces = []
    for prefix in range(4):
        pieces.append(
            jnp.dot(
                weights[prefix].T,
                image_part[:, bounds[prefix] : bounds[prefix + 1]],
                preferred_element_type=jnp.float32,
            )
        )
    return jnp.concatenate(pieces, 1)


def body(pooled, text_embed, head_weight, logit_scale, logit_bias, partner):
    block_rows = pooled.shape[0]
    factor = 1.0 / math.sqrt(block_rows * lax.axis_size("row") * lax.axis_size("col"))
    embedding = jnp.dot(pooled, head_weight, preferred_element_type=jnp.float32).astype(
        jnp.bfloat16
    )
    local_ids = jnp.arange(block_rows, dtype=jnp.int32)
    positive = (partner[0][:, None] == local_ids[None, :]).astype(jnp.float32)
    empty = jnp.zeros((block_rows, block_rows), jnp.float32)
    weights, bounds = segment_weights(
        embedding, text_embed, positive, logit_scale, logit_bias, factor
    )
    own_image = image_side(weights, bounds, text_embed)
    own_text = text_side(weights, bounds, embedding)
    behind = shifted(text_embed, "row", 1)
    weights, bounds = segment_weights(embedding, behind, empty, logit_scale, logit_bias, factor)
    cross_image = image_side(weights, bounds, behind)
    cross_text = text_side(weights, bounds, embedding)
    returned = shifted(cross_text.astype(jnp.bfloat16), "row", -1).astype(cross_text.dtype)
    text_grad = own_text + returned
    image_grad = own_image + cross_image
    column_block = lax.all_to_all(
        image_grad.astype(jnp.bfloat16), "col", split_axis=1, concat_axis=0, tiled=True
    ).astype(image_grad.dtype)
    group_rows = lax.all_gather(pooled, "col", axis=0, tiled=True)
    block_term = jnp.dot(
        group_rows.astype(jnp.float32).T, column_block, precision=lax.Precision.HIGHEST
    )
    head_grad = lax.psum_scatter(block_term, "row", scatter_dimension=0, tiled=True)
    return (text_grad, head_grad)


def dot_nt(left, right):
    return lax.dot_general(
        left, right, (((1,), (1,)), ((), ())), preferred_element_type=jnp.float32
    )


def dot_nn(left, right):
    return jnp.dot(left, right, preferred_element_type=jnp.float32)


def aligned(low_end, high_end):
    return low_end // LANES * LANES, -(-high_end // LANES) * LANES


def weights_of(score_of, positive, scale_ref, bias_ref, factor):
    running = None
    level_grads = []
    for prefix in range(4):
        part = score_of(prefix)
        running = part if running is None else running + part
        gate = jax.nn.sigmoid(scale_ref[prefix] * running + bias_ref[prefix])
        if positive is not None:
            gate = gate - positive
        level_grads.append(gate * factor)
    weights = [None] * 4
    carried = None
    for prefix in range(3, -1, -1):
        term = scale_ref[prefix] * level_grads[prefix]
        carried = term if carried is None else carried + term
        weights[prefix] = carried.astype(jnp.bfloat16)
    return weights


def by_tile(piece_of, bounds, store):
    pieces = []
    for q in range(4):
        start, stop = aligned(bounds[q], bounds[q + 1])
        pieces.append((start, stop, piece_of(q, start, stop)))
    for tile in range(bounds[4] // LANES):
        base = tile * LANES
        value = None
        for q in range(4):
            start, stop, piece = pieces[q]
            if start <= base < stop:
                here = piece[:, base - start : base - start + LANES]
                if value is None:
                    value = here
                else:
                    lane = lax.broadcasted_iota(jnp.int32, here.shape, 1)
                    value = jnp.where(lane < bounds[q] - base, value, here)
        store(base, value)


def kernel(
    n_row,
    n_col,
    factor,
    plan,
    pooled_hbm,
    text_hbm,
    weight_hbm,
    scale_hbm,
    bias_hbm,
    partner_hbm,
    text_grad_ref,
    head_grad_ref,
    pooled_ref,
    text_ref,
    weight_ref,
    scale_ref,
    bias_ref,
    partner_ref,
    load_sem,
    image_sum,
    cross_text,
    text_back,
    text_behind,
    pooled_t,
    pooled_in,
    embed,
    masked,
    image_out,
    image_in,
    total,
    x_out,
    x_in,
    z_out,
    z_in,
    near_send,
    near_recv,
    pool_send,
    pool_recv,
    image_send,
    image_recv,
    x_send,
    x_recv,
    z_send,
    z_recv,
):
    window, image_tail, out_tail = plan
    rows, width = pooled_hbm.shape
    head_rows = width // n_row
    head_cols = width // n_col
    tiles = head_cols // LANES
    tail = head_cols % LANES
    bounds = [0, width // 8, width // 4, width // 2, width]
    row = lax.axis_index("row")
    col = lax.axis_index("col")
    half = n_row // 2
    y = row // half
    x = row // 2 % 2
    core = row % 2
    pair = col % 2
    side = col // 2

    other_core = row + 1 - 2 * core
    over_y = (row + half) % n_row
    over_y_other = over_y + 1 - 2 * core
    over_x = row + 2 - 4 * x
    over_z = col + 1 - 2 * pair
    far_z = (col + 2) % n_col

    barrier = pltpu.get_barrier_semaphore()
    peers = (
        ((row + 1) % n_row, col),
        ((row + n_row - 1) % n_row, col),
        (over_x, col),
        (over_y, col),
        (over_y_other, col),
        (row, over_z),
        (other_core, over_z),
        (over_y, over_z),
        (row, far_z),
    )
    for peer in peers:
        pl.semaphore_signal(barrier, inc=1, device_id=peer, device_id_type=MESH)

    loads = [
        pltpu.make_async_copy(src, dst, load_sem.at[n])
        for n, (src, dst) in enumerate(
            (
                (pooled_hbm, pooled_ref),
                (weight_hbm, weight_ref),
                (text_hbm, text_ref),
                (scale_hbm, scale_ref),
                (bias_hbm, bias_ref),
                (partner_hbm, partner_ref),
            )
        )
    ]
    for load in loads:
        load.start()

    def remote(src, dst, send, recv, device):
        return pltpu.make_async_remote_copy(
            src_ref=src,
            dst_ref=dst,
            send_sem=send,
            recv_sem=recv,
            device_id=device,
            device_id_type=MESH,
        )

    behind_copy = remote(
        text_hbm, text_behind, near_send.at[0], near_recv.at[0], ((row + 1) % n_row, col)
    )
    back_copy = remote(
        cross_text,
        text_back,
        near_send.at[1],
        near_recv.at[1],
        ((row + n_row - 1) % n_row, col),
    )
    pl.semaphore_wait(barrier, len(peers))
    behind_copy.start()
    loads[0].wait()

    for tile in range(width // LANES):
        part = pooled_ref[:, pl.ds(tile * LANES, LANES)].T
        at = tile * LANES
        while at < (tile + 1) * LANES:
            block = at // head_rows
            stop = min((block + 1) * head_rows, (tile + 1) * LANES)
            pooled_t[block // 2, block % 2, pl.ds(at - block * head_rows, stop - at), :] = part[
                at - tile * LANES : stop - tile * LANES
            ]
            at = stop

    def pool_copy(src, slot, device):
        wait = {2: 1, 3: 2}.get(slot, 0)
        return remote(src, pooled_in.at[slot], pool_send, pool_recv.at[wait], device)

    def pooled_for(half_y, half_core):
        return pooled_t.at[pl.ds(2 * half_y, 2), half_core]

    pool_copies = {
        4: pool_copy(pooled_for(y, core), 4, (row, over_z)),
        5: pool_copy(pooled_for(y, 1 - core), 5, (other_core, over_z)),
        2: pool_copy(pooled_for(1 - y, core), 2, (over_y, col)),
        3: pool_copy(pooled_for(1 - y, 1 - core), 3, (over_y_other, col)),
        1: pool_copy(pooled_for(y, 1 - core), 1, (other_core, col)),
    }
    for copy in pool_copies.values():
        copy.start()
    for slot in (6, 7):
        pool_copies[slot] = pool_copy(pooled_in.at[slot - 4], slot, (row, over_z))
    pooled_in[0] = pooled_t[pl.ds(2 * y, 2), core]

    def fill_embed(source):
        at = 0
        for q in range(4):
            start, stop = aligned(bounds[q], bounds[q + 1])
            at += stop - start
        step = 3 * LANES if width % (3 * LANES) == 0 else LANES
        for base in range(0, width, step):
            part = dot_nn(source[...], weight_ref[:, pl.ds(base, step)])
            embed[:, pl.ds(base, step)] = part.astype(jnp.bfloat16)
        at = 0
        for q in range(4):
            start, stop = aligned(bounds[q], bounds[q + 1])
            part = embed[:, pl.ds(start, stop - start)].astype(jnp.float32)
            lane = lax.broadcasted_iota(jnp.int32, part.shape, 1) + start
            keep = (lane >= bounds[q]) & (lane < bounds[q + 1])
            masked[:, pl.ds(at, stop - start)] = jnp.where(keep, part, 0.0).astype(
                jnp.bfloat16
            )
            at += stop - start

    def masked_part(q):
        at = 0
        for before in range(q):
            start, stop = aligned(bounds[before], bounds[before + 1])
            at += stop - start
        start, stop = aligned(bounds[q], bounds[q + 1])
        return masked[:, pl.ds(at, stop - start)]

    def text_part(ref, q):
        start, stop = aligned(bounds[q], bounds[q + 1])
        return ref[:, pl.ds(start, stop - start)]

    loads[1].wait()
    fill_embed(pooled_ref)
    for load in loads[2:]:
        load.wait()
    text_id = lax.broadcasted_iota(jnp.int32, (rows, rows), 0)
    positive = (text_id == partner_ref[...]).astype(jnp.float32).T
    own = weights_of(
        lambda q: dot_nt(masked_part(q), text_part(text_ref, q)),
        positive,
        scale_ref,
        bias_ref,
        factor,
    )

    def own_image_piece(q, start, stop):
        return dot_nn(own[q], text_ref[:, pl.ds(start, stop - start)])

    def keep_image(base, value):
        image_sum[:, pl.ds(base, LANES)] = value

    by_tile(own_image_piece, bounds, keep_image)

    def folded(value, kept):
        lane = lax.broadcasted_iota(jnp.int32, value.shape, 1)
        value = jnp.where(lane < tail, value, 0.0)
        joined = value[:kept]
        for n in range(1, value.shape[0] // kept):
            joined = joined + pltpu.roll(value[n * kept : (n + 1) * kept], n * tail, 1)
        return joined

    def block_of(turn, parity):
        return parity + 2 * (side if turn == 1 else 1 - side)

    def image_copy(src, slot, turn, device):
        return remote(
            src,
            image_in.at[turn, slot],
            image_send,
            image_recv.at[slot // 2 if slot % 2 == 0 else 0, turn],
            device,
        )

    image_copies = {}
    for turn in range(2):
        mine = image_out.at[block_of(turn, pair)]
        theirs = image_out.at[block_of(turn, 1 - pair)]
        held = [image_in.at[turn, slot] for slot in range(8)]
        image_copies[4, turn] = image_copy(theirs, 4, turn, (row, over_z))
        image_copies[2, turn] = image_copy(mine, 2, turn, (over_y, col))
        image_copies[1, turn] = image_copy(mine, 1, turn, (other_core, col))
        image_copies[6, turn] = image_copy(theirs, 6, turn, (over_y, over_z))
        for slot in (3, 5, 7):
            image_copies[slot, turn] = image_copy(held[slot - 1], slot, turn, (other_core, col))

    def cross_phase():
        behind_copy.wait_recv()
        cross = weights_of(
            lambda q: dot_nt(masked_part(q), text_part(text_behind, q)),
            None,
            scale_ref,
            bias_ref,
            factor,
        )

        def image_piece(q, start, stop):
            return dot_nn(cross[q], text_behind[:, pl.ds(start, stop - start)])

        def add_image(base, value):
            lanes = pl.ds(base, LANES)
            image_sum[:, lanes] = image_sum[:, lanes] + value

        by_tile(image_piece, bounds, add_image)
        def pack(block):
            first = block * head_cols // LANES * LANES
            offset = block * head_cols - first
            part = image_sum[:, pl.ds(pl.multiple_of(first, LANES), window)]
            part = pltpu.roll(part, (window - offset) % window, 1)
            for n in range(tiles):
                image_out[block, pl.ds(n * rows, rows), :] = part[
                    :, n * LANES : (n + 1) * LANES
                ].astype(jnp.bfloat16)
            if tail:
                last = folded(part[:, tiles * LANES : (tiles + 1) * LANES], image_tail)
                image_out[block, pl.ds(tiles * rows, image_tail), :] = last.astype(jnp.bfloat16)

        for turn in range(2):
            for slot in (4, 2):
                pack(block_of(turn, 1 - pair if slot == 4 else pair))
                if turn == 0:
                    image_copies[slot + 2 if slot == 4 else 1, turn].start()
                    image_copies[slot, turn].start()

        def own_text_piece(q, start, stop):
            return dot_nn(own[q].T, embed[:, pl.ds(start, stop - start)])

        def store_text(base, value):
            text_grad_ref[:, pl.ds(base, LANES)] = value

        def cross_text_piece(q, start, stop):
            return dot_nn(cross[q].T, embed[:, pl.ds(start, stop - start)])

        def store_cross(base, value):
            cross_text[:, pl.ds(base, LANES)] = value.astype(jnp.bfloat16)

        by_tile(cross_text_piece, bounds, store_cross)

        @pl.when(core + x > 0)
        def _():
            back_copy.start()

        by_tile(own_text_piece, bounds, store_text)

    cross_phase()
    for slot in (6, 7):
        pool_copies[slot - 4].wait_recv()
        pool_copies[slot].start()

    def forward(slot, turn):
        image_copies[slot, turn].wait_recv()
        image_copies[slot + 1, turn].start()

    for slot in (6, 4, 2, 1):
        image_copies[slot, 1].start()

    def forward_second():
        for slot in (4, 2, 6):
            forward(slot, 1)

    forward(4, 0)
    forward(2, 0)
    for turn in range(2):
        image_in[turn, 0] = image_out[block_of(turn, pair)]
    forward(6, 0)
    several = pooled_in.at[pl.ds(0, 5)]
    remote(several, several, pool_send, pool_recv.at[0], (other_core, col)).wait_recv()

    parts = [(n * head_rows, head_rows) for n in range(tiles)]
    if tail:
        parts.append((tiles * head_rows, out_tail))

    def part_of(ref, n):
        return ref.at[pl.ds(parts[n][0], parts[n][1]), :]

    x_copies = {
        (turn, n): remote(
            part_of(x_out.at[turn], n),
            part_of(x_in.at[turn], n),
            x_send,
            x_recv.at[n if turn == 0 else len(parts)],
            (over_x, col),
        )
        for turn in range(2)
        for n in range(len(parts))
    }
    z_copies = [
        remote(part_of(z_out, n), part_of(z_in, n), z_send, z_recv, (row, far_z))
        for n in range(len(parts))
    ]

    def keep_part(turn, n, value):
        first, count = parts[n]
        for there in range(2):
            piece = value[there * head_rows : (there + 1) * head_rows]
            if n == tiles:
                piece = folded(piece, count)
            total[turn, there, pl.ds(first, count), :] = piece
        x_out[turn, pl.ds(first, count), :] = total[
            turn, 1 - x, pl.ds(first, count), :
        ].astype(jnp.bfloat16)
        x_copies[turn, n].start()

    def multiply(turn):
        several = image_in.at[turn, pl.ds(0, 4)]
        remote(
            several, several, image_send, image_recv.at[0, turn], (other_core, col)
        ).wait_recv()
        left = jnp.concatenate(
            [pooled_in[slot].reshape(2 * head_rows, rows) for slot in range(8)], 1
        )
        sides = [
            image_in[turn, :, pl.ds(n * rows, rows), :].reshape(8 * rows, LANES)
            for n in range(tiles)
        ]
        main = dot_nn(left, jnp.concatenate(sides, 1))
        for n in range(tiles):
            keep_part(turn, n, main[:, n * LANES : (n + 1) * LANES])
        if tail:
            pieces = []
            for slot in range(8):
                held = image_in[turn, slot, pl.ds(tiles * rows, image_tail), :]
                held = held.astype(jnp.float32)
                for n in range(rows // image_tail):
                    moved = pltpu.roll(held, LANES - n * tail, 1) if n else held
                    pieces.append(moved.astype(jnp.bfloat16))
            keep_part(turn, tiles, dot_nn(left, jnp.concatenate(pieces, 0)))

    multiply(0)

    @pl.when(core + x == 0)
    def _():
        back_copy.start()

    forward_second()
    for n, (first, count) in enumerate(parts):
        at = pl.ds(first, count)
        x_copies[0, n].wait_recv()
        value = total[0, x, at, :] + x_in[0, at, :].astype(jnp.float32)
        z_out[at, :] = value.astype(jnp.bfloat16)
        z_copies[n].start()

    multiply(1)
    back_copy.wait_recv()
    text_grad_ref[...] = text_grad_ref[...] + text_back[...].astype(jnp.float32)

    all_z = remote(z_out, z_in, z_send, z_recv, (row, far_z))
    remote(x_out.at[1], x_in.at[1], x_send, x_recv.at[len(parts)], (over_x, col)).wait_recv()
    all_z.wait_recv()
    for n, (first, count) in enumerate(parts):
        at = pl.ds(first, count)
        value = total[1, x, at, :] + x_in[1, at, :].astype(jnp.float32)
        value = value + z_in[at, :].astype(jnp.float32)
        if n < tiles:
            head_grad_ref[:, pl.ds(n * LANES, LANES)] = value
        else:
            for j in range(head_rows // count):
                here = pltpu.roll(value, LANES - j * tail, 1) if j else value
                head_grad_ref[pl.ds(j * count, count), pl.ds(tiles * LANES, tail)] = here[:, :tail]

    behind_copy.wait_send()
    back_copy.wait_send()
    several = pooled_in.at[pl.ds(0, 7)]
    remote(several, several, pool_send, pool_recv.at[0], (other_core, col)).wait_send()
    several = image_in.at[:, pl.ds(0, 7)]
    remote(several, several, image_send, image_recv.at[0, 0], (other_core, col)).wait_send()
    remote(x_out, x_in, x_send, x_recv.at[0], (over_x, col)).wait_send()
    all_z.wait_send()


def deliver(text_grad, head_grad):
    def move(text_from, head_from, text_to, head_to, sems):
        copies = [
            pltpu.make_async_copy(text_from, text_to, sems.at[0]),
            pltpu.make_async_copy(head_from, head_to, sems.at[1]),
        ]
        for copy in copies:
            copy.start()
        for copy in copies:
            copy.wait()

    vmem = pl.BlockSpec(memory_space=pltpu.VMEM)
    anywhere = pl.BlockSpec(memory_space=pl.ANY)
    return pl.pallas_call(
        move,
        out_shape=(
            jax.ShapeDtypeStruct(text_grad.shape, text_grad.dtype),
            jax.ShapeDtypeStruct(head_grad.shape, head_grad.dtype),
        ),
        in_specs=[vmem, vmem],
        out_specs=(anywhere, anywhere),
        scratch_shapes=[pltpu.SemaphoreType.DMA((2,))],
    )(
        pltpu.with_memory_space_constraint(text_grad, pltpu.VMEM),
        pltpu.with_memory_space_constraint(head_grad, pltpu.VMEM),
    )


def fold_of(count, tail):
    fitting = [n for n in range(1, LANES // tail + 1 if tail else 2) if count % (16 * n) == 0]
    return count // max(fitting) if fitting else None


def plan_of(rows, width, n_row, n_col):
    head_rows, head_cols = width // n_row, width // n_col
    spans = [aligned(c * head_cols, (c + 1) * head_cols) for c in range(n_col)]
    window = max(stop - start for start, stop in spans)
    if head_cols < LANES or any(start + window > width for start, _ in spans):
        return None
    image_tail = fold_of(rows, head_cols % LANES)
    out_tail = fold_of(head_rows, head_cols % LANES)
    if image_tail is None or out_tail is None:
        return None
    return window, image_tail, out_tail


def fused_body(n_row, n_col, pooled, text_embed, head_weight, logit_scale, logit_bias, partner):
    rows, width = pooled.shape
    factor = 1.0 / math.sqrt(rows * n_row * n_col)
    plan = plan_of(rows, width, n_row, n_col)
    _, image_tail, out_tail = plan
    head_rows, head_cols = width // n_row, width // n_col
    tiles, ragged = head_cols // LANES, head_cols % LANES > 0
    image_rows = tiles * rows + ragged * image_tail
    out_rows = tiles * head_rows + ragged * out_tail
    parts = tiles + ragged
    bounds = [0, width // 8, width // 4, width // 2, width]
    spans = [aligned(bounds[q], bounds[q + 1]) for q in range(4)]
    masked_width = sum(stop - start for start, stop in spans)
    vmem = pl.BlockSpec(memory_space=pltpu.VMEM)
    dma = pltpu.SemaphoreType.DMA
    bf16, f32 = jnp.bfloat16, jnp.float32
    return pl.pallas_call(
        functools.partial(kernel, n_row, n_col, factor, plan),
        out_shape=(
            pltpu.VMEM((rows, width), jnp.float32),
            pltpu.VMEM((head_rows, head_cols), jnp.float32),
        ),
        in_specs=[pl.BlockSpec(memory_space=pl.ANY)] * 6,
        out_specs=(vmem, vmem),
        scratch_shapes=[
            pltpu.VMEM(pooled.shape, bf16),
            pltpu.VMEM(text_embed.shape, bf16),
            pltpu.VMEM(head_weight.shape, bf16),
            pltpu.SMEM(logit_scale.shape, f32),
            pltpu.SMEM(logit_bias.shape, f32),
            pltpu.VMEM(partner.shape, jnp.int32),
            dma((6,)),
            pltpu.VMEM((rows, width), f32),
            pltpu.VMEM((rows, width), bf16),
            pltpu.VMEM((rows, width), bf16),
            pltpu.VMEM((rows, width), bf16),
            pltpu.VMEM((n_row // 2, 2, head_rows, rows), bf16),
            pltpu.VMEM((8, 2, head_rows, rows), bf16),
            pltpu.VMEM((rows, width), bf16),
            pltpu.VMEM((rows, masked_width), bf16),
            pltpu.VMEM((n_col, image_rows, LANES), bf16),
            pltpu.VMEM((2, 8, image_rows, LANES), bf16),
            pltpu.VMEM((2, 2, out_rows, LANES), f32),
            pltpu.VMEM((2, out_rows, LANES), bf16),
            pltpu.VMEM((2, out_rows, LANES), bf16),
            pltpu.VMEM((out_rows, LANES), bf16),
            pltpu.VMEM((out_rows, LANES), bf16),
            dma((2,)),
            dma((2,)),
            dma,
            dma((3,)),
            dma,
            dma((4, 2)),
            dma,
            dma((parts + 1,)),
            dma,
            dma,
        ],
        compiler_params=pltpu.CompilerParams(collective_id=0, has_side_effects=True),
    )(pooled, text_embed, head_weight, logit_scale, logit_bias, partner)


def per_device(n_row, n_col):
    def run(pooled, text_embed, head_weight, logit_scale, logit_bias, partner):
        rows, width = pooled.shape
        fused = (
            n_row == 2**3
            and n_col == 2**2
            and rows == LANES
            and width % LANES == 0
            and width % (16 * n_row) == 0
            and width % n_col == 0
            and plan_of(rows, width, n_row, n_col) is not None
        )
        args = (pooled, text_embed, head_weight, logit_scale, logit_bias, partner)
        return deliver(*fused_body(n_row, n_col, *args)) if fused else body(*args)

    return run


def solution(mesh):
    in_specs = (
        P(("row", "col"), None),
        P(("row", "col"), None),
        P(),
        P(),
        P(),
        P(("row", "col"), None),
    )
    out_specs = (P(("row", "col"), None), P("row", "col"))
    run = per_device(mesh.shape["row"], mesh.shape["col"])
    return jax.shard_map(run, mesh=mesh, in_specs=in_specs, out_specs=out_specs, check_vma=False)
```
